256 devices in a mesh: section: 8 (over y, core), leaf: 32 (over x, z).
Axes of the slice: x: 4, y: 4, z: 8, core: 2. Of those that a mesh axis runs over, the one named last changes fastest.
Arguments:
- state_map: float32 [8, 512, 512], P('section'), may hold values from -0.05303301 to 1.053033
- input_map: float32 [8, 512, 256], P('section'), may hold values from -0.25 to 0.25
- cost_state: float32 [8, 1, 32, 512], P('section', None, 'leaf'), may hold values from 0.5 to 5
- cost_input: float32 [8, 1, 32, 256], P('section', None, 'leaf'), may hold values from 0.5 to 5
- terminal: float32 [8, 1, 32, 512], P('section', None, 'leaf'), may hold values from 0.5 to 5
- prob_num: int32 [8, 1, 32], P('section', None, 'leaf'), may hold values from 56 to 64
- crosses: int32 [8, 1, 32], P('section', None, 'leaf'), may hold values 0 or 1
- root_state_map: float32 [512, 512], replicated, may hold values from -0.05303301 to 1.053033
- root_input_map: float32 [512, 256], replicated, may hold values from -0.25 to 0.25
- root_cost_input: float32 [1, 256], replicated, may hold values from 0.5 to 5
- root_terminal: float32 [1, 512], replicated, may hold values from 0.5 to 5
Outputs:
- hessian: float32 [8, 1, 32, 512, 512], P('section', None, 'leaf')
- gain: float32 [8, 1, 32, 256, 512], P('section', None, 'leaf')
- root_gain: float32 [1, 256, 512], P(None, 'section')
The draws below stay inside these ranges and needn't reach their ends.
Inputs may be any that keep to these rules, and one draw needn't show every extreme that they name: `prob_num`: branch probability numerators in 64ths.
All inputs are finite; a program needn't handle non-finite values. No bound on the sum of `crosses` on one device may be relied on, other than what follows from the above.
Results may differ from the reference program's by a relative error of at most 0.00021.
Values sent between devices are 32-bit elements; how exact they have to be, the bound alone decides.
A program may use at most 128 MiB of HBM per device.

```python
import math
import jax
import jax.numpy as jnp
from jax import lax

NX = 512
NU = 256
FRONTS = 1
SECTIONS = 8
GROUPS = 32


def near_identity(key, shape):
    spread = 0.3 * NX ** (-0.5)
    noise = jnp.clip(jax.random.normal(key, shape, jnp.float32), -4.0, 4.0) * spread
    return jnp.eye(NX, dtype=jnp.float32) + noise


def draw_state_map(key, part):
    return near_identity(jax.random.fold_in(key, 11), (SECTIONS, NX, NX))


def draw_root_state_map(key, part):
    return near_identity(jax.random.fold_in(key, 13), (NX, NX))


def plant(values, own_key, smallest, largest):
    longest = values.shape.index(max(values.shape))
    spots = []
    for shift in (0, 1):
        where = [jax.random.randint(jax.random.fold_in(own_key, axis), (), 0, length) for axis, length in enumerate(values.shape)]
        where[longest] = (where[longest] + shift) % values.shape[longest]
        spots.append(tuple(where))
    return values.at[spots[0]].set(smallest).at[spots[1]].set(largest)


def block_scale(own_key, dims, split, low, high):
    level, own = 1.0, jax.random.fold_in(own_key, 6)
    for position, parts in split:
        steps = jnp.exp(jax.random.uniform(jax.random.fold_in(own, position), (parts,), jnp.float32, low / len(split), high / len(split)))
        level = level * jnp.repeat(steps, dims[position] // parts).reshape([-1 if axis == position else 1 for axis in range(len(dims))])
    return level


def scatter_about(stream_key, extent, deviation, bound, shards=(), held_as=jnp.bfloat16):
    drawn = jax.random.normal(stream_key, extent, jnp.float32) * deviation
    if len(shards) > 0:
        drawn = block_scale(stream_key, extent, shards, -0.22, 0.18) * drawn
    return jnp.clip(drawn, min=-bound, max=bound).astype(held_as)


def setup_inputs(seed: int = 0) -> dict:
    seeds = jax.random.split(jax.random.key(seed), 12)
    state_map = draw_state_map(jax.random.fold_in(seeds[11], 71), 0)
    input_map = scatter_about(seeds[1], (SECTIONS, NX, NU), NX ** -0.5, 0.25, ((0, 8),), jnp.float32)
    cost_state = jnp.clip(jnp.exp(math.log(5.0) - 2.3025851 * jax.random.uniform(seeds[2], (SECTIONS, FRONTS, GROUPS, NX), jnp.float32) ** block_scale(seeds[2], (SECTIONS, FRONTS, GROUPS, NX), ((0, 8), (2, 32)), -0.2, 0.2)), 0.5, 5.0)
    cost_input = jnp.clip(jnp.exp(math.log(5.0) - 2.3025851 * jax.random.uniform(seeds[3], (SECTIONS, FRONTS, GROUPS, NU), jnp.float32) ** block_scale(seeds[3], (SECTIONS, FRONTS, GROUPS, NU), ((0, 8), (2, 32)), -0.2, 0.2)), 0.5, 5.0)
    terminal = jnp.clip(jnp.exp(math.log(5.0) - 2.3025851 * jax.random.uniform(seeds[4], (SECTIONS, FRONTS, GROUPS, NX), jnp.float32) ** block_scale(seeds[4], (SECTIONS, FRONTS, GROUPS, NX), ((0, 8), (2, 32)), -0.2, 0.2)), 0.5, 5.0)
    prob_num = plant(jax.random.randint(seeds[5], (SECTIONS, FRONTS, GROUPS), 56, 65), jax.random.fold_in(seeds[5], 1), 56, 64).astype(jnp.int32)
    crosses = plant((jax.random.randint(seeds[6], (SECTIONS, FRONTS, GROUPS), 0, 2) < 1).astype(jnp.int32), jax.random.fold_in(seeds[6], 1), 0, 1)
    root_state_map = draw_root_state_map(jax.random.fold_in(seeds[11], 71), 0)
    root_input_map = scatter_about(seeds[8], (NX, NU), NX ** -0.5, 0.25, (), jnp.float32)
    root_cost_input = jnp.clip(jnp.exp(jax.random.uniform(seeds[9], (FRONTS, NU), jnp.float32, math.log(0.5), math.log(5.0))), 0.5, 5.0)
    root_terminal = jnp.clip(jnp.exp(jax.random.uniform(seeds[10], (FRONTS, NX), jnp.float32, math.log(0.5), math.log(5.0))), 0.5, 5.0)
    return dict(state_map=state_map, input_map=input_map, cost_state=cost_state, cost_input=cost_input, terminal=terminal, prob_num=prob_num, crosses=crosses, root_state_map=root_state_map, root_input_map=root_input_map, root_cost_input=root_cost_input, root_terminal=root_terminal)


def finish(hess_xx, hess_ux, hess_uu):
    precise = lax.Precision.HIGHEST
    factor = jnp.linalg.cholesky(hess_uu)
    scaled = lax.linalg.triangular_solve(factor, hess_ux, left_side=True, lower=True)
    feedback = -lax.linalg.triangular_solve(factor, scaled, left_side=True, lower=True, transpose_a=True)
    hessian = hess_xx - jnp.dot(scaled.T, scaled, precision=precise)
    return (hessian, feedback)

def riccati(expected, state_map, input_map, cost_state, cost_input):
    precise = lax.Precision.HIGHEST
    exp_state = jnp.dot(expected, state_map, precision=precise)
    exp_input = jnp.dot(expected, input_map, precision=precise)
    hess_xx = jnp.dot(state_map.T, exp_state, precision=precise) + jnp.diag(cost_state)
    hess_ux = jnp.dot(input_map.T, exp_state, precision=precise)
    hess_uu = jnp.dot(input_map.T, exp_input, precision=precise) + jnp.diag(cost_input)
    return finish(hess_xx, hess_ux, hess_uu)

def reference(state_map, input_map, cost_state, cost_input, terminal, prob_num, crosses, root_state_map, root_input_map, root_cost_input, root_terminal):
    batched = jax.vmap(jax.vmap(riccati, in_axes=(0, None, None, 0, 0)), in_axes=(0, None, None, 0, 0))
    identity = jnp.eye(NX, dtype=jnp.float32)
    incoming = jnp.zeros((FRONTS, GROUPS, NX, NX), jnp.float32)
    hess_list = []
    gain_list = []
    weighted = incoming
    for section_id in reversed(range(SECTIONS)):
        expected = terminal[section_id][:, :, :, None] * identity + incoming
        hess_new, gain_new = batched(expected, state_map[section_id], input_map[section_id], cost_state[section_id], cost_input[section_id])
        hess_list.append(hess_new)
        gain_list.append(gain_new)
        weighted = (prob_num[section_id].astype(jnp.float32) / 64.0)[:, :, None, None] * hess_new
        far_part = crosses[section_id].astype(jnp.float32)[:, :, None, None] * weighted
        incoming = weighted - far_part + jnp.roll(far_part, 1, axis=1)
    root_total = root_terminal[:, :, None] * identity + jnp.sum(weighted, axis=1)
    root_batched = jax.vmap(riccati, in_axes=(0, None, None, 0, 0))
    zero_cost = jnp.zeros((FRONTS, NX), jnp.float32)
    root_hess, root_feedback = root_batched(root_total, root_state_map, root_input_map, zero_cost, root_cost_input)
    hessian = jnp.stack(hess_list[::-1], axis=0)
    gain = jnp.stack(gain_list[::-1], axis=0)
    return (hessian, gain, root_feedback)
```

```python
import functools

import jax
import jax.numpy as jnp
from jax import lax
from jax.experimental import pallas as pl
from jax.experimental.pallas import tpu as pltpu
from jax.sharding import PartitionSpec as P

F32, BF16 = jnp.float32, jnp.bfloat16
MESH = pl.DeviceIdType.MESH
VMEM = pltpu.VMEM
CONTRACT = (((1,), (0,)), ((), ()))
CONTRACT_ROWS = (((0,), (0,)), ((), ()))


def split(x):
    high = x.astype(BF16)
    return high, (x - high.astype(F32)).astype(BF16)


def dot_one(a, b, dims=CONTRACT):
    return lax.dot_general(a, b, dims, preferred_element_type=F32)


def dot_split(a, b, dims=CONTRACT):
    return dot_one(a[0], b[0], dims) + (dot_one(a[0], b[1], dims) + dot_one(a[1], b[0], dims))


def dot3(a, b, dims=CONTRACT):
    return dot_split(split(a), split(b), dims)


def lanes(x, j):
    return jnp.broadcast_to(x[:, j : j + 1], (8, 128))


def rows(x, k):
    return jnp.broadcast_to(x[k : k + 1, :], (8, 128))


def inverse128(a):
    groups = 16
    lane = lax.broadcasted_iota(jnp.int32, (8, 128), 1)
    row = lax.broadcasted_iota(jnp.int32, (8, 128), 0)
    masks = [row == k for k in range(8)]
    held = [a[8 * g : 8 * g + 8, :] for g in range(groups)]
    for t in range(groups):
        off = 8 * t
        inside = (lane >= off) & (lane < off + 8)
        top = held[t]
        cols = [lanes(top, off + j) for j in range(8)]
        top = jnp.where(inside, jnp.where(lane - off == row, 1.0, 0.0), top)
        for k in range(8):
            pivot = 1.0 / rows(cols[k], k)
            lead = rows(top, k) * pivot
            factor = jnp.where(masks[k], 0.0, cols[k])
            top = jnp.where(masks[k], lead, top - factor * lead)
            for j in range(k + 1, 8):
                lead_j = rows(cols[j], k) * pivot
                cols[j] = jnp.where(masks[k], lead_j, cols[j] - factor * lead_j)
        out = [jnp.where(inside, 0.0, held[g]) for g in range(groups)]
        for k in range(8):
            lead = rows(top, k)
            for g in range(groups):
                if g != t:
                    out[g] = out[g] - lanes(held[g], off + k) * lead
        out[t] = top
        held = out
    return jnp.concatenate(held, axis=0)


def solve(huu, hux, inv):
    a12, a21 = huu[0:128, 128:256], huu[128:256, 0:128]
    hux1 = hux[0:128]
    first = split(inv(huu[0:128, 0:128]))
    t12 = dot_split(first, split(a12))
    th = dot_split(first, split(hux1))
    a21s = split(a21)
    second = split(inv(huu[128:256, 128:256] - dot_split(a21s, split(t12))))
    rest = hux[128:256] - dot_split(a21s, split(th))
    g2 = dot_split(second, split(rest))
    g1 = th - dot3(t12, g2)
    return hux1, th, rest, g2, g1


def eye_times(vector, size):
    r = lax.broadcasted_iota(jnp.int32, (size, size), 0)
    c = lax.broadcasted_iota(jnp.int32, (size, size), 1)
    return jnp.where(r == c, jnp.broadcast_to(vector, (size, size)), 0.0)


def chain_kernel(
    sections, groups, prob, crosses, state_map, input_map, cost_state, cost_input, terminal,
    hess_ref, gain_ref,
    own_in, far_in, own_out, far_out,
    m_s, n_s, mt_s, nt_s, e_s, ym_s, yn_s, hux_ref, z_ref, x_ref, inv_ref,
    own_send, own_recv, far_send, far_recv,
):
    s = lax.axis_index("section")
    g = lax.axis_index("leaf")
    up, down = lax.rem(s + sections - 1, sections), lax.rem(s + 1, sections)
    after, before = lax.rem(g + 1, groups), lax.rem(g + groups - 1, groups)
    parents = ({"section": up, "leaf": g}, {"section": up, "leaf": after})
    children = ({"section": down, "leaf": g}, {"section": down, "leaf": before})

    barrier = pltpu.get_barrier_semaphore()
    for other in parents + children:
        pl.semaphore_signal(barrier, inc=1, device_id=other, device_id_type=MESH)
    pl.semaphore_wait(barrier, 4)

    def slabs(src, dst, send, recv, device):
        out = []
        for i in range(4):
            part = (pl.ds(128 * i, 128), pl.ds(0, 128 * (i + 1)))
            out.append(
                pltpu.make_async_remote_copy(
                    src_ref=src.at[part], dst_ref=dst.at[part], send_sem=send.at[i], recv_sem=recv.at[i],
                    device_id=device, device_id_type=MESH,
                )
            )
        return out

    own_copies = slabs(own_out, own_in, own_send, own_recv, parents[0])
    far_copies = slabs(far_out, far_in, far_send, far_recv, parents[1])

    for i in range(4):
        block = slice(128 * i, 128 * (i + 1))
        value = state_map[block, :]
        m_s[0, block, :], m_s[1, block, :] = split(value)
        mt_s[0, :, block], mt_s[1, :, block] = split(value.T)
        value = input_map[block, :]
        n_s[0, block, :], n_s[1, block, :] = split(value)
        nt_s[0, :, block], nt_s[1, :, block] = split(value.T)

    @pl.when(s == sections - 1)
    def _():
        own_in[...] = jnp.zeros_like(own_in)
        far_in[...] = jnp.zeros_like(far_in)

    for i in range(4):
        @pl.when(s < sections - 1)
        def _():
            far_copies[i].wait_recv()
            own_copies[i].wait_recv()

        rowb = slice(128 * i, 128 * (i + 1))
        for j in range(i + 1):
            colb = slice(128 * j, 128 * (j + 1))
            block = own_in[rowb, colb] + far_in[rowb, colb]
            if i == j:
                block = block + eye_times(terminal[0:1, rowb], 128)
            e_s[0, rowb, colb], e_s[1, rowb, colb] = split(block)
            if i != j:
                e_s[0, colb, rowb], e_s[1, colb, rowb] = split(block.T)

    e = (e_s[0], e_s[1])
    yn_s[0], yn_s[1] = split(dot_split(e, (n_s[0], n_s[1])))
    for j in range(2):
        colb = slice(256 * j, 256 * (j + 1))
        ym_s[0, :, colb], ym_s[1, :, colb] = split(dot_split(e, (m_s[0, :, colb], m_s[1, :, colb])))
    nt, mt = (nt_s[0], nt_s[1]), (mt_s[0], mt_s[1])
    huu = dot_split(nt, (yn_s[0], yn_s[1])) + eye_times(cost_input[0:1, :], 256)
    for j in range(2):
        colb = slice(256 * j, 256 * (j + 1))
        ym = (ym_s[0, :, colb], ym_s[1, :, colb])
        hux_ref[:, colb] = dot_split(nt, ym)
        hess_ref[:, colb] = dot_split(mt, ym)
    for i in range(4):
        block = slice(128 * i, 128 * (i + 1))
        hess_ref[block, block] = hess_ref[block, block] + eye_times(cost_state[0:1, block], 128)

    def inv(a):
        return inverse128(a)

    hux1, th, rest, g2, g1 = solve(huu, hux_ref[...], inv)
    x_ref[0, 0:128, :], x_ref[1, 0:128, :] = split(hux1)
    x_ref[0, 128:256, :], x_ref[1, 128:256, :] = split(rest)
    z_ref[0, 0:128, :], z_ref[1, 0:128, :] = split(th)
    z_ref[0, 128:256, :], z_ref[1, 128:256, :] = split(g2)
    weight = prob[0].astype(F32) / 64.0
    crossing = crosses[0].astype(F32)
    far_weight = weight * crossing
    own_weight = weight - far_weight
    for j in range(2):
        colb = slice(256 * j, 256 * (j + 1))
        z = (z_ref[0, :, colb], z_ref[1, :, colb])
        hess_ref[:, colb] = hess_ref[:, colb] - dot_split((x_ref[0], x_ref[1]), z, CONTRACT_ROWS)

    for i in range(4):
        rowb = slice(128 * i, 128 * (i + 1))
        colb = slice(0, 128 * (i + 1))
        value = hess_ref[rowb, colb]
        far_out[rowb, colb] = value * far_weight
        own_out[rowb, colb] = value * own_weight

        @pl.when(s > 0)
        def _():
            far_copies[i].start()
            own_copies[i].start()

    gain_ref[0:128, :] = -g1
    gain_ref[128:256, :] = -g2

    @pl.when(s > 0)
    def _():
        for i in range(4):
            far_copies[i].wait_send()
            own_copies[i].wait_send()


def root_kernel(expected_input, state_map, input_map, cost_input, gain_ref):
    y = split(expected_input[...])
    huu = dot_split(split(input_map[...].T), y) + eye_times(cost_input[0:1, :], 256)
    hux = dot_split(y, split(state_map[...]), CONTRACT_ROWS)
    hux1, th, rest, g2, g1 = solve(huu, hux, inverse128)
    gain_ref[0:128, :] = -g1
    gain_ref[128:256, :] = -g2


def on_device(
    state_map, input_map, cost_state, cost_input, terminal, prob_num, crosses,
    root_state_map, root_input_map, root_cost_input, root_terminal,
):
    sections, groups = lax.axis_size("section"), lax.axis_size("leaf")
    section, leaf = lax.axis_index("section"), lax.axis_index("leaf")
    nx, nu = input_map.shape[1], input_map.shape[2]
    vmem, smem = pl.BlockSpec(memory_space=pltpu.VMEM), pl.BlockSpec(memory_space=pltpu.SMEM)
    dma = pltpu.SemaphoreType.DMA((4,))
    hess, gain = pl.pallas_call(
        functools.partial(chain_kernel, sections, groups),
        out_shape=(jax.ShapeDtypeStruct((nx, nx), F32), jax.ShapeDtypeStruct((nu, nx), F32)),
        in_specs=[smem, smem] + [vmem] * 5,
        out_specs=(vmem, vmem),
        scratch_shapes=[VMEM((nx, nx), F32)] * 4
        + [
            VMEM((2, nx, nx), BF16), VMEM((2, nx, nu), BF16), VMEM((2, nx, nx), BF16), VMEM((2, nu, nx), BF16),
            VMEM((2, nx, nx), BF16), VMEM((2, nx, nx), BF16), VMEM((2, nx, nu), BF16),
            VMEM((nu, nx), F32), VMEM((2, nu, nx), BF16), VMEM((2, nu, nx), BF16), VMEM((128, 128), F32),
        ]
        + [dma] * 4,
        compiler_params=pltpu.CompilerParams(collective_id=0, has_side_effects=True, vmem_limit_bytes=60 << 20),
    )(
        prob_num.reshape(1), crosses.reshape(1), state_map[0], input_map[0],
        cost_state.reshape(1, nx), cost_input.reshape(1, nu), terminal.reshape(1, nx),
    )
    precise = lax.Precision.HIGHEST
    weight = jnp.where(section == 0, prob_num[0, 0, 0].astype(F32) / 64.0, 0.0)
    part = jnp.dot(hess * weight, root_input_map, precision=precise)
    total = lax.psum(part, ("section", "leaf")) + root_terminal[0][:, None] * root_input_map
    root = pl.pallas_call(
        root_kernel,
        out_shape=jax.ShapeDtypeStruct((nu, nx), F32),
        in_specs=[vmem] * 4,
        out_specs=vmem,
        compiler_params=pltpu.CompilerParams(vmem_limit_bytes=60 << 20),
    )(total, root_state_map, root_input_map, root_cost_input)
    mine = lax.dynamic_slice_in_dim(root, section * (nu // sections), nu // sections, 0)
    return hess[None, None, None], gain[None, None, None], mine[None]


def solution(mesh):
    in_specs = (
        P("section", None, None), P("section", None, None), P("section", None, "leaf", None),
        P("section", None, "leaf", None), P("section", None, "leaf", None), P("section", None, "leaf"),
        P("section", None, "leaf"), P(), P(), P(), P(),
    )
    out_specs = (
        P("section", None, "leaf", None, None), P("section", None, "leaf", None, None), P(None, "section", None),
    )
    return jax.shard_map(on_device, mesh=mesh, in_specs=in_specs, out_specs=out_specs, check_vma=False)
```

```python
import functools

import jax
import jax.numpy as jnp
from jax import lax
from jax.experimental import pallas as pl
from jax.experimental.pallas import tpu as pltpu
from jax.sharding import PartitionSpec as P

F32, BF16 = jnp.float32, jnp.bfloat16
MESH = pl.DeviceIdType.MESH
VMEM = pltpu.VMEM
CONTRACT = (((1,), (0,)), ((), ()))
CONTRACT_ROWS = (((0,), (0,)), ((), ()))


def split(x):
    high = x.astype(BF16)
    return high, (x - high.astype(F32)).astype(BF16)


def dot_one(a, b, dims=CONTRACT):
    return lax.dot_general(a, b, dims, preferred_element_type=F32)


def dot_split(a, b, dims=CONTRACT):
    return dot_one(a[0], b[0], dims) + (dot_one(a[0], b[1], dims) + dot_one(a[1], b[0], dims))


def dot3(a, b, dims=CONTRACT):
    return dot_split(split(a), split(b), dims)


def lanes(x, j):
    return jnp.broadcast_to(x[:, j : j + 1], (8, 128))


def rows(x, k):
    return jnp.broadcast_to(x[k : k + 1, :], (8, 128))


def inverse128(a):
    groups = 16
    lane = lax.broadcasted_iota(jnp.int32, (8, 128), 1)
    row = lax.broadcasted_iota(jnp.int32, (8, 128), 0)
    masks = [row == k for k in range(8)]
    held = [a[8 * g : 8 * g + 8, :] for g in range(groups)]
    for t in range(groups):
        off = 8 * t
        inside = (lane >= off) & (lane < off + 8)
        top = held[t]
        cols = [lanes(top, off + j) for j in range(8)]
        top = jnp.where(inside, jnp.where(lane - off == row, 1.0, 0.0), top)
        for k in range(8):
            pivot = 1.0 / rows(cols[k], k)
            lead = rows(top, k) * pivot
            factor = jnp.where(masks[k], 0.0, cols[k])
            top = jnp.where(masks[k], lead, top - factor * lead)
            for j in range(k + 1, 8):
                lead_j = rows(cols[j], k) * pivot
                cols[j] = jnp.where(masks[k], lead_j, cols[j] - factor * lead_j)
        out = [jnp.where(inside, 0.0, held[g]) for g in range(groups)]
        for k in range(8):
            lead = rows(top, k)
            for g in range(groups):
                if g != t:
                    out[g] = out[g] - lanes(held[g], off + k) * lead
        out[t] = top
        held = out
    return jnp.concatenate(held, axis=0)


def solve(huu, hux, inv):
    a12, a21 = huu[0:128, 128:256], huu[128:256, 0:128]
    hux1 = hux[0:128]
    first = split(inv(huu[0:128, 0:128]))
    t12 = dot_split(first, split(a12))
    th = dot_split(first, split(hux1))
    a21s = split(a21)
    second = split(inv(huu[128:256, 128:256] - dot_split(a21s, split(t12))))
    rest = hux[128:256] - dot_split(a21s, split(th))
    g2 = dot_split(second, split(rest))
    g1 = th - dot3(t12, g2)
    return hux1, th, rest, g2, g1


def eye_times(vector, size):
    r = lax.broadcasted_iota(jnp.int32, (size, size), 0)
    c = lax.broadcasted_iota(jnp.int32, (size, size), 1)
    return jnp.where(r == c, jnp.broadcast_to(vector, (size, size)), 0.0)


def chain_kernel(
    sections, groups, prob, crosses, state_map, input_map, cost_state, cost_input, terminal,
    root_state_map, root_input_map, root_cost_input, root_terminal,
    hess_hbm, gain_hbm, root_ref,
    hess_ref, gain_ref, own_in, far_in, own_out, far_out,
    m_s, n_s, mt_s, nt_s, e_s, ym_s, yn_s, hux_ref, z_ref, x_ref,
    mr_ref, nr_ref, mr_s, nr_s, nrt_s, tail_ref, part_ref, parts_in, full_ref, slice_ref,
    own_send, own_recv, far_send, far_recv,
    part_send, part_recv, full_send, full_recv, slice_send, slice_recv, local,
):
    s = lax.axis_index("section")
    g = lax.axis_index("leaf")
    up, down = lax.rem(s + sections - 1, sections), lax.rem(s + 1, sections)
    after, before = lax.rem(g + 1, groups), lax.rem(g + groups - 1, groups)
    parents = ({"section": up, "leaf": g}, {"section": up, "leaf": after})
    children = ({"section": down, "leaf": g}, {"section": down, "leaf": before})

    barrier = pltpu.get_barrier_semaphore()
    for other in parents + children:
        pl.semaphore_signal(barrier, inc=1, device_id=other, device_id_type=MESH)

    @pl.when(s == 0)
    def _():
        @pl.loop(1, groups)
        def _(d):
            pl.semaphore_signal(
                barrier, inc=1, device_id={"leaf": lax.rem(g + d, groups)}, device_id_type=MESH
            )

        @pl.loop(1, sections)
        def _(d):
            pl.semaphore_signal(barrier, inc=1, device_id={"section": d}, device_id_type=MESH)

    @pl.when(s > 0)
    def _():
        pl.semaphore_signal(barrier, inc=1, device_id={"section": 0}, device_id_type=MESH)

    pl.semaphore_wait(barrier, jnp.where(s == 0, 4 + (groups - 1) + (sections - 1), 5))

    def slabs(src, dst, send, recv, device):
        out = []
        for i in range(4):
            part = (pl.ds(128 * i, 128), pl.ds(0, 128 * (i + 1)))
            out.append(
                pltpu.make_async_remote_copy(
                    src_ref=src.at[part], dst_ref=dst.at[part], send_sem=send.at[i], recv_sem=recv.at[i],
                    device_id=device, device_id_type=MESH,
                )
            )
        return out

    own_copies = slabs(own_out, own_in, own_send, own_recv, parents[0])
    far_copies = slabs(far_out, far_in, far_send, far_recv, parents[1])

    for i in range(4):
        block = slice(128 * i, 128 * (i + 1))
        value = state_map[block, :]
        m_s[0, block, :], m_s[1, block, :] = split(value)
        mt_s[0, :, block], mt_s[1, :, block] = split(value.T)
        value = input_map[block, :]
        n_s[0, block, :], n_s[1, block, :] = split(value)
        nt_s[0, :, block], nt_s[1, :, block] = split(value.T)

    @pl.when(s == 0)
    def _():
        fetch_m = pltpu.make_async_copy(root_state_map, mr_ref, local.at[0])
        fetch_n = pltpu.make_async_copy(root_input_map, nr_ref, local.at[1])
        fetch_m.start()
        fetch_n.start()
        fetch_m.wait()
        fetch_n.wait()
        for i in range(4):
            block = slice(128 * i, 128 * (i + 1))
            mr_s[0, block, :], mr_s[1, block, :] = split(mr_ref[block, :])
            value = nr_ref[block, :]
            nr_s[0, block, :], nr_s[1, block, :] = split(value)
            nrt_s[0, :, block], nrt_s[1, :, block] = split(value.T)
            column = jnp.sum(eye_times(root_terminal[0:1, block], 128), axis=1, keepdims=True)
            tail_ref[block, :] = column * value

    @pl.when(s == sections - 1)
    def _():
        own_in[...] = jnp.zeros_like(own_in)
        far_in[...] = jnp.zeros_like(far_in)

    for i in range(4):
        @pl.when(s < sections - 1)
        def _():
            far_copies[i].wait_recv()
            own_copies[i].wait_recv()

        rowb = slice(128 * i, 128 * (i + 1))
        for j in range(i + 1):
            colb = slice(128 * j, 128 * (j + 1))
            block = own_in[rowb, colb] + far_in[rowb, colb]
            if i == j:
                block = block + eye_times(terminal[0:1, rowb], 128)
            e_s[0, rowb, colb], e_s[1, rowb, colb] = split(block)
            if i != j:
                e_s[0, colb, rowb], e_s[1, colb, rowb] = split(block.T)

    e = (e_s[0], e_s[1])
    yn_s[0], yn_s[1] = split(dot_split(e, (n_s[0], n_s[1])))
    for j in range(2):
        colb = slice(256 * j, 256 * (j + 1))
        ym_s[0, :, colb], ym_s[1, :, colb] = split(dot_split(e, (m_s[0, :, colb], m_s[1, :, colb])))
    nt, mt = (nt_s[0], nt_s[1]), (mt_s[0], mt_s[1])
    huu = dot_split(nt, (yn_s[0], yn_s[1])) + eye_times(cost_input[0:1, :], 256)
    for j in range(2):
        colb = slice(256 * j, 256 * (j + 1))
        hux_ref[:, colb] = dot_split(nt, (ym_s[0, :, colb], ym_s[1, :, colb]))
    for i in range(2):
        rowb = slice(256 * i, 256 * (i + 1))
        colb = slice(0, 256 * (i + 1))
        hess_ref[rowb, colb] = dot_split(
            (mt_s[0, rowb, :], mt_s[1, rowb, :]), (ym_s[0, :, colb], ym_s[1, :, colb])
        )

    hux1, th, rest, g2, g1 = solve(huu, hux_ref[...], inverse128)
    x_ref[0, 0:128, :], x_ref[1, 0:128, :] = split(hux1)
    x_ref[0, 128:256, :], x_ref[1, 128:256, :] = split(rest)
    z_ref[0, 0:128, :], z_ref[1, 0:128, :] = split(th)
    z_ref[0, 128:256, :], z_ref[1, 128:256, :] = split(g2)
    weight = prob[0].astype(F32) / 64.0
    crossing = crosses[0].astype(F32)
    far_weight = weight * crossing
    own_weight = weight - far_weight

    for i in range(2):
        rowc = slice(256 * i, 256 * (i + 1))
        colc = slice(0, 256 * (i + 1))
        update = dot_split(
            (x_ref[0, :, rowc], x_ref[1, :, rowc]), (z_ref[0, :, colc], z_ref[1, :, colc]), CONTRACT_ROWS
        )
        for h in range(2):
            k = 2 * i + h
            rowb, colb = slice(128 * k, 128 * (k + 1)), slice(0, 128 * (k + 1))
            value = hess_ref[rowb, colb] - update[128 * h : 128 * (h + 1), 0 : 128 * (k + 1)]
            hess_ref[rowb, colb] = value
            diagonal = value[:, 128 * k :] + eye_times(cost_state[0:1, rowb], 128)
            hess_ref[rowb, rowb] = diagonal
            if k > 0:
                below = value[:, 0 : 128 * k]
                far_out[rowb, 0 : 128 * k] = below * far_weight
                own_out[rowb, 0 : 128 * k] = below * own_weight
            far_out[rowb, rowb] = diagonal * far_weight
            own_out[rowb, rowb] = diagonal * own_weight
        for k in (2 * i, 2 * i + 1):
            @pl.when(s > 0)
            def _():
                far_copies[k].start()
                own_copies[k].start()

    for i in range(4):
        rowb = slice(128 * i, 128 * (i + 1))
        for j in range(i):
            colb = slice(128 * j, 128 * (j + 1))
            hess_ref[colb, rowb] = hess_ref[rowb, colb].T
    gain_ref[0:128, :] = -g1
    gain_ref[128:256, :] = -g2

    hess_write = pltpu.make_async_copy(hess_ref, hess_hbm, local.at[2])
    gain_write = pltpu.make_async_copy(gain_ref, gain_hbm, local.at[3])
    hess_write.start()
    gain_write.start()

    @pl.when(s > 0)
    def _():
        for i in range(4):
            far_copies[i].wait_send()
            own_copies[i].wait_send()

    chunk = part_ref.shape[0] // groups

    def part_copy(peer, sender):
        return pltpu.make_async_remote_copy(
            src_ref=part_ref.at[pl.ds(pl.multiple_of(chunk * peer, chunk), chunk), :], dst_ref=parts_in.at[sender],
            send_sem=part_send.at[peer], recv_sem=part_recv.at[sender],
            device_id={"leaf": peer}, device_id_type=MESH,
        )

    def full_copy(peer, sender):
        here = (pl.ds(pl.multiple_of(chunk * sender, chunk), chunk), slice(None))
        return pltpu.make_async_remote_copy(
            src_ref=full_ref.at[here], dst_ref=full_ref.at[here],
            send_sem=full_send.at[peer], recv_sem=full_recv.at[sender],
            device_id={"leaf": peer}, device_id_type=MESH,
        )

    def slice_copy(other):
        return pltpu.make_async_remote_copy(
            src_ref=gain_ref.at[pl.ds(pl.multiple_of(32 * other, 32), 32), :], dst_ref=slice_ref,
            send_sem=slice_send.at[other], recv_sem=slice_recv.at[0],
            device_id={"section": other}, device_id_type=MESH,
        )

    @pl.when(s == 0)
    def _():
        nr = (nr_s[0], nr_s[1])
        for i in range(2):
            rowb = slice(256 * i, 256 * (i + 1))
            part_ref[rowb, :] = dot_split(split(hess_ref[rowb, :]), nr) * weight

        @pl.loop(1, groups)
        def _(d):
            part_copy(lax.rem(g + d, groups), g).start()

        mine = pl.ds(pl.multiple_of(chunk * g, chunk), chunk)
        parts_in[g] = part_ref[mine, :]

        @pl.loop(1, groups)
        def _(d):
            peer = lax.rem(g + d, groups)
            part_copy(peer, peer).wait_recv()

        total = tail_ref[mine, :]
        for i in range(groups):
            total = total + parts_in[i]
        full_ref[mine, :] = total

        @pl.loop(1, groups)
        def _(d):
            full_copy(lax.rem(g + d, groups), g).start()

        gain_write.wait()

        @pl.loop(1, groups)
        def _(d):
            peer = lax.rem(g + d, groups)
            full_copy(peer, peer).wait_recv()

        y = split(full_ref[...])
        root_huu = dot_split((nrt_s[0], nrt_s[1]), y) + eye_times(root_cost_input[0:1, :], 256)
        root_hux = dot_split(y, (mr_s[0], mr_s[1]), CONTRACT_ROWS)
        _, _, _, low, high = solve(root_huu, root_hux, inverse128)
        gain_ref[0:128, :] = -high
        gain_ref[128:256, :] = -low

        @pl.loop(1, sections)
        def _(d):
            slice_copy(d).start()

        root_ref[...] = gain_ref[0:32, :]

        @pl.loop(1, groups)
        def _(d):
            peer = lax.rem(g + d, groups)
            part_copy(peer, g).wait_send()
            full_copy(peer, g).wait_send()

        @pl.loop(1, sections)
        def _(d):
            slice_copy(d).wait_send()

    @pl.when(s > 0)
    def _():
        gain_write.wait()
        slice_copy(s).wait_recv()
        root_ref[...] = slice_ref[...]

    hess_write.wait()


def on_device(
    state_map, input_map, cost_state, cost_input, terminal, prob_num, crosses,
    root_state_map, root_input_map, root_cost_input, root_terminal,
):
    sections, groups = lax.axis_size("section"), lax.axis_size("leaf")
    nx, nu = input_map.shape[1], input_map.shape[2]
    vmem, smem = pl.BlockSpec(memory_space=pltpu.VMEM), pl.BlockSpec(memory_space=pltpu.SMEM)
    hbm = pl.BlockSpec(memory_space=pl.ANY)
    dma = pltpu.SemaphoreType.DMA
    hess, gain, mine = pl.pallas_call(
        functools.partial(chain_kernel, sections, groups),
        out_shape=(
            jax.ShapeDtypeStruct((nx, nx), F32),
            jax.ShapeDtypeStruct((nu, nx), F32),
            jax.ShapeDtypeStruct((nu // sections, nx), F32),
        ),
        in_specs=[smem, smem] + [vmem] * 5 + [hbm, hbm, vmem, vmem],
        out_specs=(hbm, hbm, vmem),
        scratch_shapes=[VMEM((nx, nx), F32), VMEM((nu, nx), F32)]
        + [VMEM((nx, nx), F32)] * 4
        + [
            VMEM((2, nx, nx), BF16), VMEM((2, nx, nu), BF16), VMEM((2, nx, nx), BF16), VMEM((2, nu, nx), BF16),
            VMEM((2, nx, nx), BF16), VMEM((2, nx, nx), BF16), VMEM((2, nx, nu), BF16),
            VMEM((nu, nx), F32), VMEM((2, nu, nx), BF16), VMEM((2, nu, nx), BF16),
            VMEM((nx, nx), F32), VMEM((nx, nu), F32), VMEM((2, nx, nx), BF16), VMEM((2, nx, nu), BF16),
            VMEM((2, nu, nx), BF16), VMEM((nx, nu), F32), VMEM((nx, nu), F32),
            VMEM((groups, nx // groups, nu), F32), VMEM((nx, nu), F32), VMEM((nu // sections, nx), F32),
        ]
        + [dma((4,))] * 4
        + [dma((groups,))] * 4
        + [dma((sections,)), dma((1,)), dma((4,))],
        compiler_params=pltpu.CompilerParams(collective_id=0, has_side_effects=True, vmem_limit_bytes=60 << 20),
    )(
        prob_num.reshape(1), crosses.reshape(1), state_map[0], input_map[0],
        cost_state.reshape(1, nx), cost_input.reshape(1, nu), terminal.reshape(1, nx),
        root_state_map, root_input_map, root_cost_input, root_terminal,
    )
    return hess[None, None, None], gain[None, None, None], mine[None]


def solution(mesh):
    in_specs = (
        P("section", None, None), P("section", None, None), P("section", None, "leaf", None),
        P("section", None, "leaf", None), P("section", None, "leaf", None), P("section", None, "leaf"),
        P("section", None, "leaf"), P(), P(), P(), P(),
    )
    out_specs = (
        P("section", None, "leaf", None, None), P("section", None, "leaf", None, None), P(None, "section", None),
    )
    return jax.shard_map(on_device, mesh=mesh, in_specs=in_specs, out_specs=out_specs, check_vma=False)
```

```python
import functools

import jax
import jax.numpy as jnp
from jax import lax
from jax.experimental import pallas as pl
from jax.experimental.pallas import tpu as pltpu
from jax.sharding import PartitionSpec as P

F32, BF16 = jnp.float32, jnp.bfloat16
PIECES = ((0, 264), (264, 256), (520, 256), (776, 264))
CONTENT = (
    (("pair", 0, 1), ("one", 1, 0)), (("one", 2, 0), ("one", 2, 1)), (("one", 3, 0), ("one", 3, 1)),
    (("pair", 2, 3), ("one", 3, 2)),
)
MESH = pl.DeviceIdType.MESH
VMEM = pltpu.VMEM
CONTRACT = (((1,), (0,)), ((), ()))
CONTRACT_ROWS = (((0,), (0,)), ((), ()))


def split(x):
    high = x.astype(BF16)
    return high, (x - high.astype(F32)).astype(BF16)


def dot_one(a, b, dims=CONTRACT):
    return lax.dot_general(a, b, dims, preferred_element_type=F32)


def dot_split(a, b, dims=CONTRACT):
    return dot_one(a[0], b[0], dims) + (dot_one(a[0], b[1], dims) + dot_one(a[1], b[0], dims))


def dot3(a, b, dims=CONTRACT):
    return dot_split(split(a), split(b), dims)


def lanes(x, j):
    return jnp.broadcast_to(x[:, j : j + 1], (8, 128))


def rows(x, k):
    return jnp.broadcast_to(x[k : k + 1, :], (8, 128))


def inverse128(a):
    groups = 16
    lane = lax.broadcasted_iota(jnp.int32, (8, 128), 1)
    row = lax.broadcasted_iota(jnp.int32, (8, 128), 0)
    masks = [row == k for k in range(8)]
    held = [a[8 * g : 8 * g + 8, :] for g in range(groups)]
    for t in range(groups):
        off = 8 * t
        inside = (lane >= off) & (lane < off + 8)
        top = held[t]
        cols = [lanes(top, off + j) for j in range(8)]
        top = jnp.where(inside, jnp.where(lane - off == row, 1.0, 0.0), top)
        for k in range(8):
            pivot = 1.0 / rows(cols[k], k)
            lead = rows(top, k) * pivot
            factor = jnp.where(masks[k], 0.0, cols[k])
            top = jnp.where(masks[k], lead, top - factor * lead)
            for j in range(k + 1, 8):
                lead_j = rows(cols[j], k) * pivot
                cols[j] = jnp.where(masks[k], lead_j, cols[j] - factor * lead_j)
        out = [jnp.where(inside, 0.0, held[g]) for g in range(groups)]
        for k in range(8):
            lead = rows(top, k)
            for g in range(groups):
                if g != t:
                    out[g] = out[g] - lanes(held[g], off + k) * lead
        out[t] = top
        held = out
    return jnp.concatenate(held, axis=0)


def solve(huu, hux, inv):
    a12, a21 = huu[0:128, 128:256], huu[128:256, 0:128]
    hux1 = hux[0:128]
    first = split(inv(huu[0:128, 0:128]))
    t12 = dot_split(first, split(a12))
    th = dot_split(first, split(hux1))
    a21s = split(a21)
    second = split(inv(huu[128:256, 128:256] - dot_split(a21s, split(t12))))
    rest = hux[128:256] - dot_split(a21s, split(th))
    g2 = dot_split(second, split(rest))
    g1 = th - dot3(t12, g2)
    return hux1, th, rest, g2, g1


def eye_times(vector, size):
    r = lax.broadcasted_iota(jnp.int32, (size, size), 0)
    c = lax.broadcasted_iota(jnp.int32, (size, size), 1)
    return jnp.where(r == c, jnp.broadcast_to(vector, (size, size)), 0.0)


def chain_kernel(
    sections, groups, prob, crosses, state_map, input_map, cost_state, cost_input, terminal,
    root_state_map, root_input_map, root_cost_input, root_terminal,
    hess_hbm, gain_hbm, root_ref,
    hess_ref, gain_ref, own_in, far_in, peer_in, own_out, far_out,
    m_s, n_s, mt_s, nt_s, e_s, ym_s, yn_s, hux_ref, z_ref, x_ref,
    mr_ref, nr_ref, mr_s, nr_s, nrt_s, tail_ref, part_ref, parts_in, full_ref, slice_ref,
    own_send, own_recv, far_send, far_recv, peer_send, peer_recv,
    part_send, part_recv, full_send, full_recv, slice_send, slice_recv, local,
):
    s = lax.axis_index("section")
    g = lax.axis_index("leaf")
    up, down = lax.rem(s + sections - 1, sections), lax.rem(s + 1, sections)
    after, before = lax.rem(g + 1, groups), lax.rem(g + groups - 1, groups)
    parents = ({"section": up, "leaf": g}, {"section": up, "leaf": after})
    children = ({"section": down, "leaf": g}, {"section": down, "leaf": before})
    siblings = ({"leaf": after}, {"leaf": before})
    far_side = lax.rem(s, 2) == 1

    barrier = pltpu.get_barrier_semaphore()
    for other in parents + children + siblings:
        pl.semaphore_signal(barrier, inc=1, device_id=other, device_id_type=MESH)

    @pl.when(s == 0)
    def _():
        @pl.loop(1, groups)
        def _(d):
            pl.semaphore_signal(
                barrier, inc=1, device_id={"leaf": lax.rem(g + d, groups)}, device_id_type=MESH
            )

        @pl.loop(1, sections)
        def _(d):
            pl.semaphore_signal(barrier, inc=1, device_id={"section": d}, device_id_type=MESH)

    @pl.when(s > 0)
    def _():
        pl.semaphore_signal(barrier, inc=1, device_id={"section": 0}, device_id_type=MESH)

    pl.semaphore_wait(barrier, jnp.where(s == 0, 6 + (groups - 1) + (sections - 1), 7))

    def pieces(src, dst, send, recv, device):
        return [
            pltpu.make_async_remote_copy(
                src_ref=src.at[pl.ds(start, size)], dst_ref=dst.at[pl.ds(start, size)],
                send_sem=send.at[i], recv_sem=recv.at[i], device_id=device, device_id_type=MESH,
            )
            for i, (start, size) in enumerate(PIECES)
        ]

    own_copies = pieces(own_out, own_in, own_send, own_recv, parents[0])
    far_copies = pieces(far_out, far_in, far_send, far_recv, parents[1])
    peer_copies = pieces(far_out, peer_in, peer_send, peer_recv, siblings[0])

    for i in range(4):
        block = slice(128 * i, 128 * (i + 1))
        value = state_map[block, :]
        m_s[0, block, :], m_s[1, block, :] = split(value)
        mt_s[0, :, block], mt_s[1, :, block] = split(value.T)
        value = input_map[block, :]
        n_s[0, block, :], n_s[1, block, :] = split(value)
        nt_s[0, :, block], nt_s[1, :, block] = split(value.T)

    @pl.when(s == 0)
    def _():
        fetch_m = pltpu.make_async_copy(root_state_map, mr_ref, local.at[0])
        fetch_n = pltpu.make_async_copy(root_input_map, nr_ref, local.at[1])
        fetch_m.start()
        fetch_n.start()
        fetch_m.wait()
        fetch_n.wait()
        for i in range(4):
            block = slice(128 * i, 128 * (i + 1))
            mr_s[0, block, :], mr_s[1, block, :] = split(mr_ref[block, :])
            value = nr_ref[block, :]
            nr_s[0, block, :], nr_s[1, block, :] = split(value)
            nrt_s[0, :, block], nrt_s[1, :, block] = split(value.T)
            column = jnp.sum(eye_times(root_terminal[0:1, block], 128), axis=1, keepdims=True)
            tail_ref[block, :] = column * value

    @pl.when(s == sections - 1)
    def _():
        own_in[...] = jnp.zeros_like(own_in)

    @pl.when(far_side)
    def _():
        far_in[...] = jnp.zeros_like(far_in)

    r = lax.broadcasted_iota(jnp.int32, (128, 128), 0)
    c = lax.broadcasted_iota(jnp.int32, (128, 128), 1)

    def put(i, j, block):
        rowb, colb = slice(128 * i, 128 * (i + 1)), slice(128 * j, 128 * (j + 1))
        if i == j:
            block = block + eye_times(terminal[0:1, rowb], 128)
        e_s[0, rowb, colb], e_s[1, rowb, colb] = split(block)
        if i != j:
            e_s[0, colb, rowb], e_s[1, colb, rowb] = split(block.T)

    for p, (start, size) in enumerate(PIECES):
        @pl.when(s < sections - 1)
        def _():
            own_copies[p].wait_recv()

            @pl.when(jnp.logical_not(far_side))
            def _():
                far_copies[p].wait_recv()

        for h, (kind, i, j) in enumerate(CONTENT[p]):
            here = slice(start + 128 * h, start + 128 * (h + 1))
            block = own_in[here, :] + far_in[here, :]
            if kind == "pair":
                spare = slice(start + 256, start + 257)
                line = own_in[spare, :] + far_in[spare, :]
                turned = block.T
                put(i, i, jnp.where(r >= c, block, turned))
                put(j, j, jnp.where(r < c, block, jnp.where(r > c, turned, line)))
            else:
                put(i, j, block)

    e = (e_s[0], e_s[1])
    yn_s[0], yn_s[1] = split(dot_split(e, (n_s[0], n_s[1])))
    for j in range(2):
        colb = slice(256 * j, 256 * (j + 1))
        ym_s[0, :, colb], ym_s[1, :, colb] = split(dot_split(e, (m_s[0, :, colb], m_s[1, :, colb])))
    nt, mt = (nt_s[0], nt_s[1]), (mt_s[0], mt_s[1])
    huu = dot_split(nt, (yn_s[0], yn_s[1])) + eye_times(cost_input[0:1, :], 256)
    for j in range(2):
        colb = slice(256 * j, 256 * (j + 1))
        hux_ref[:, colb] = dot_split(nt, (ym_s[0, :, colb], ym_s[1, :, colb]))
    for i in range(2):
        rowb = slice(256 * i, 256 * (i + 1))
        colb = slice(0, 256 * (i + 1))
        hess_ref[rowb, colb] = dot_split(
            (mt_s[0, rowb, :], mt_s[1, rowb, :]), (ym_s[0, :, colb], ym_s[1, :, colb])
        )

    hux1, th, rest, g2, g1 = solve(huu, hux_ref[...], inverse128)
    x_ref[0, 0:128, :], x_ref[1, 0:128, :] = split(hux1)
    x_ref[0, 128:256, :], x_ref[1, 128:256, :] = split(rest)
    z_ref[0, 0:128, :], z_ref[1, 0:128, :] = split(th)
    z_ref[0, 128:256, :], z_ref[1, 128:256, :] = split(g2)
    weight = prob[0].astype(F32) / 64.0
    crossing = crosses[0].astype(F32)
    far_weight = weight * crossing
    own_weight = weight - far_weight

    def load(start, value):
        far_out[start : start + value.shape[0], :] = value * far_weight
        own_out[start : start + value.shape[0], :] = value * own_weight

    for i in range(2):
        rowc = slice(256 * i, 256 * (i + 1))
        colc = slice(0, 256 * (i + 1))
        update = dot_split(
            (x_ref[0, :, rowc], x_ref[1, :, rowc]), (z_ref[0, :, colc], z_ref[1, :, colc]), CONTRACT_ROWS
        )
        for h in range(2):
            k = 2 * i + h
            rowb, colb = slice(128 * k, 128 * (k + 1)), slice(0, 128 * (k + 1))
            hess_ref[rowb, colb] = hess_ref[rowb, colb] - update[128 * h : 128 * (h + 1), 0 : 128 * (k + 1)]
            hess_ref[rowb, rowb] = hess_ref[rowb, rowb] + eye_times(cost_state[0:1, rowb], 128)
        for p in ((0,), (1, 2, 3))[i]:
            start = PIECES[p][0]
            for h, (kind, a, b) in enumerate(CONTENT[p]):
                block = hess_ref[128 * a : 128 * (a + 1), 128 * b : 128 * (b + 1)]
                if kind == "pair":
                    first = hess_ref[128 * a : 128 * (a + 1), 128 * a : 128 * (a + 1)]
                    second = hess_ref[128 * b : 128 * (b + 1), 128 * b : 128 * (b + 1)]
                    block = jnp.where(r >= c, first, second)
                    line = jnp.sum(jnp.where(r == c, second, 0.0), axis=0, keepdims=True)
                    load(start + 256, jnp.broadcast_to(line, (8, 128)))
                load(start + 128 * h, block)

            @pl.when(far_side)
            def _():
                far_copies[p].start()
                own_copies[p].start()

            @pl.when(jnp.logical_not(far_side) & (s > 0))
            def _():
                peer_copies[p].start()

    @pl.when(jnp.logical_not(far_side) & (s > 0))
    def _():
        for p, (start, size) in enumerate(PIECES):
            peer_copies[p].wait_recv()
            here = slice(start, start + size)
            own_out[here, :] = own_out[here, :] + peer_in[here, :]
            own_copies[p].start()

    for i in range(4):
        rowb = slice(128 * i, 128 * (i + 1))
        for j in range(i):
            colb = slice(128 * j, 128 * (j + 1))
            hess_ref[colb, rowb] = hess_ref[rowb, colb].T
    gain_ref[0:128, :] = -g1
    gain_ref[128:256, :] = -g2

    hess_write = pltpu.make_async_copy(hess_ref, hess_hbm, local.at[2])
    gain_write = pltpu.make_async_copy(gain_ref, gain_hbm, local.at[3])
    hess_write.start()
    gain_write.start()

    @pl.when(s > 0)
    def _():
        for copy in own_copies:
            copy.wait_send()

        @pl.when(far_side)
        def _():
            for copy in far_copies:
                copy.wait_send()

        @pl.when(jnp.logical_not(far_side))
        def _():
            for copy in peer_copies:
                copy.wait_send()

    chunk = part_ref.shape[0] // groups

    def part_copy(peer, sender):
        return pltpu.make_async_remote_copy(
            src_ref=part_ref.at[pl.ds(pl.multiple_of(chunk * peer, chunk), chunk), :], dst_ref=parts_in.at[sender],
            send_sem=part_send.at[peer], recv_sem=part_recv.at[sender],
            device_id={"leaf": peer}, device_id_type=MESH,
        )

    def full_copy(peer, sender):
        here = (pl.ds(pl.multiple_of(chunk * sender, chunk), chunk), slice(None))
        return pltpu.make_async_remote_copy(
            src_ref=full_ref.at[here], dst_ref=full_ref.at[here],
            send_sem=full_send.at[peer], recv_sem=full_recv.at[sender],
            device_id={"leaf": peer}, device_id_type=MESH,
        )

    def slice_copy(other):
        return pltpu.make_async_remote_copy(
            src_ref=gain_ref.at[pl.ds(pl.multiple_of(32 * other, 32), 32), :], dst_ref=slice_ref,
            send_sem=slice_send.at[other], recv_sem=slice_recv.at[0],
            device_id={"section": other}, device_id_type=MESH,
        )

    @pl.when(s == 0)
    def _():
        nr = (nr_s[0], nr_s[1])
        for i in range(2):
            rowb = slice(256 * i, 256 * (i + 1))
            part_ref[rowb, :] = dot_split(split(hess_ref[rowb, :]), nr) * weight

        @pl.loop(1, groups)
        def _(d):
            part_copy(lax.rem(g + d, groups), g).start()

        mine = pl.ds(pl.multiple_of(chunk * g, chunk), chunk)
        parts_in[g] = part_ref[mine, :]

        @pl.loop(1, groups)
        def _(d):
            peer = lax.rem(g + d, groups)
            part_copy(peer, peer).wait_recv()

        total = tail_ref[mine, :]
        for i in range(groups):
            total = total + parts_in[i]
        full_ref[mine, :] = total

        @pl.loop(1, groups)
        def _(d):
            full_copy(lax.rem(g + d, groups), g).start()

        gain_write.wait()

        @pl.loop(1, groups)
        def _(d):
            peer = lax.rem(g + d, groups)
            full_copy(peer, peer).wait_recv()

        y = split(full_ref[...])
        root_huu = dot_split((nrt_s[0], nrt_s[1]), y) + eye_times(root_cost_input[0:1, :], 256)
        root_hux = dot_split(y, (mr_s[0], mr_s[1]), CONTRACT_ROWS)
        _, _, _, low, high = solve(root_huu, root_hux, inverse128)
        gain_ref[0:128, :] = -high
        gain_ref[128:256, :] = -low

        @pl.loop(1, sections)
        def _(d):
            slice_copy(d).start()

        root_ref[...] = gain_ref[0:32, :]

        @pl.loop(1, groups)
        def _(d):
            peer = lax.rem(g + d, groups)
            part_copy(peer, g).wait_send()
            full_copy(peer, g).wait_send()

        @pl.loop(1, sections)
        def _(d):
            slice_copy(d).wait_send()

    @pl.when(s > 0)
    def _():
        gain_write.wait()
        slice_copy(s).wait_recv()
        root_ref[...] = slice_ref[...]

    hess_write.wait()


def on_device(
    state_map, input_map, cost_state, cost_input, terminal, prob_num, crosses,
    root_state_map, root_input_map, root_cost_input, root_terminal,
):
    sections, groups = lax.axis_size("section"), lax.axis_size("leaf")
    nx, nu = input_map.shape[1], input_map.shape[2]
    vmem, smem = pl.BlockSpec(memory_space=pltpu.VMEM), pl.BlockSpec(memory_space=pltpu.SMEM)
    hbm = pl.BlockSpec(memory_space=pl.ANY)
    dma = pltpu.SemaphoreType.DMA
    hess, gain, mine = pl.pallas_call(
        functools.partial(chain_kernel, sections, groups),
        out_shape=(
            jax.ShapeDtypeStruct((nx, nx), F32),
            jax.ShapeDtypeStruct((nu, nx), F32),
            jax.ShapeDtypeStruct((nu // sections, nx), F32),
        ),
        in_specs=[smem, smem] + [vmem] * 5 + [hbm, hbm, vmem, vmem],
        out_specs=(hbm, hbm, vmem),
        scratch_shapes=[VMEM((nx, nx), F32), VMEM((nu, nx), F32)]
        + [VMEM((1040, 128), F32)] * 5
        + [
            VMEM((2, nx, nx), BF16), VMEM((2, nx, nu), BF16), VMEM((2, nx, nx), BF16), VMEM((2, nu, nx), BF16),
            VMEM((2, nx, nx), BF16), VMEM((2, nx, nx), BF16), VMEM((2, nx, nu), BF16),
            VMEM((nu, nx), F32), VMEM((2, nu, nx), BF16), VMEM((2, nu, nx), BF16),
            VMEM((nx, nx), F32), VMEM((nx, nu), F32), VMEM((2, nx, nx), BF16), VMEM((2, nx, nu), BF16),
            VMEM((2, nu, nx), BF16), VMEM((nx, nu), F32), VMEM((nx, nu), F32),
            VMEM((groups, nx // groups, nu), F32), VMEM((nx, nu), F32), VMEM((nu // sections, nx), F32),
        ]
        + [dma((4,))] * 6
        + [dma((groups,))] * 4
        + [dma((sections,)), dma((1,)), dma((4,))],
        compiler_params=pltpu.CompilerParams(collective_id=0, has_side_effects=True, vmem_limit_bytes=60 << 20),
    )(
        prob_num.reshape(1), crosses.reshape(1), state_map[0], input_map[0],
        cost_state.reshape(1, nx), cost_input.reshape(1, nu), terminal.reshape(1, nx),
        root_state_map, root_input_map, root_cost_input, root_terminal,
    )
    return hess[None, None, None], gain[None, None, None], mine[None]


def solution(mesh):
    in_specs = (
        P("section", None, None), P("section", None, None), P("section", None, "leaf", None),
        P("section", None, "leaf", None), P("section", None, "leaf", None), P("section", None, "leaf"),
        P("section", None, "leaf"), P(), P(), P(), P(),
    )
    out_specs = (
        P("section", None, "leaf", None, None), P("section", None, "leaf", None, None), P(None, "section", None),
    )
    return jax.shard_map(on_device, mesh=mesh, in_specs=in_specs, out_specs=out_specs, check_vma=False)
```

```python
import functools

import jax
import jax.numpy as jnp
from jax import lax
from jax.experimental import pallas as pl
from jax.experimental.pallas import tpu as pltpu
from jax.sharding import PartitionSpec as P

F32, BF16 = jnp.float32, jnp.bfloat16
PIECES = ((0, 264), (264, 256), (520, 256), (776, 264))
CONTENT = (
    (("pair", 0, 1), ("one", 1, 0)), (("one", 2, 0), ("one", 2, 1)), (("one", 3, 0), ("one", 3, 1)),
    (("pair", 2, 3), ("one", 3, 2)),
)
MESH = pl.DeviceIdType.MESH
VMEM = pltpu.VMEM
CONTRACT = (((1,), (0,)), ((), ()))
CONTRACT_ROWS = (((0,), (0,)), ((), ()))


def split(x):
    high = x.astype(BF16)
    return high, (x - high.astype(F32)).astype(BF16)


def dot_one(a, b, dims=CONTRACT):
    return lax.dot_general(a, b, dims, preferred_element_type=F32)


def dot_split(a, b, dims=CONTRACT):
    return dot_one(a[0], b[0], dims) + (dot_one(a[0], b[1], dims) + dot_one(a[1], b[0], dims))


def dot3(a, b, dims=CONTRACT):
    return dot_split(split(a), split(b), dims)


def lanes(x, j):
    return jnp.broadcast_to(x[:, j : j + 1], (8, 128))


def rows(x, k):
    return jnp.broadcast_to(x[k : k + 1, :], (8, 128))


def inverse128(a):
    groups = 16
    lane = lax.broadcasted_iota(jnp.int32, (8, 128), 1)
    row = lax.broadcasted_iota(jnp.int32, (8, 128), 0)
    masks = [row == k for k in range(8)]
    held = [a[8 * g : 8 * g + 8, :] for g in range(groups)]
    for t in range(groups):
        off = 8 * t
        inside = (lane >= off) & (lane < off + 8)
        top = held[t]
        cols = [lanes(top, off + j) for j in range(8)]
        top = jnp.where(inside, jnp.where(lane - off == row, 1.0, 0.0), top)
        for k in range(8):
            pivot = 1.0 / rows(cols[k], k)
            lead = rows(top, k) * pivot
            factor = jnp.where(masks[k], 0.0, cols[k])
            top = jnp.where(masks[k], lead, top - factor * lead)
            for j in range(k + 1, 8):
                lead_j = rows(cols[j], k) * pivot
                cols[j] = jnp.where(masks[k], lead_j, cols[j] - factor * lead_j)
        out = [jnp.where(inside, 0.0, held[g]) for g in range(groups)]
        for k in range(8):
            lead = rows(top, k)
            for g in range(groups):
                if g != t:
                    out[g] = out[g] - lanes(held[g], off + k) * lead
        out[t] = top
        held = out
    return jnp.concatenate(held, axis=0)


def solve(huu, hux, inv):
    a12, a21 = huu[0:128, 128:256], huu[128:256, 0:128]
    hux1 = hux[0:128]
    first = split(inv(huu[0:128, 0:128]))
    t12 = dot_split(first, split(a12))
    th = dot_split(first, split(hux1))
    a21s = split(a21)
    second = split(inv(huu[128:256, 128:256] - dot_split(a21s, split(t12))))
    rest = hux[128:256] - dot_split(a21s, split(th))
    g2 = dot_split(second, split(rest))
    g1 = th - dot3(t12, g2)
    return hux1, th, rest, g2, g1


def eye_times(vector, size):
    r = lax.broadcasted_iota(jnp.int32, (size, size), 0)
    c = lax.broadcasted_iota(jnp.int32, (size, size), 1)
    return jnp.where(r == c, jnp.broadcast_to(vector, (size, size)), 0.0)


def chain_kernel(
    sections, groups, prob, crosses, state_map, input_map, cost_state, cost_input, terminal,
    root_state_map, root_input_map, root_cost_input, root_terminal,
    hess_hbm, gain_hbm, root_ref,
    hess_ref, gain_ref, own_in, far_in, peer_in, own_out, far_out,
    m_s, n_s, mt_s, nt_s, e_s, ym_s, yn_s, hux_ref, z_ref, x_ref, yb_ref,
    mr_ref, nr_ref, mr_s, nr_s, nrt_s, tail_ref, part_ref, parts_in, full_ref, slices_ref, slice_ref,
    own_send, own_recv, far_send, far_recv, peer_send, peer_recv,
    part_send, part_recv, full_send, full_recv, slice_send, slice_recv, local,
):
    s = lax.axis_index("section")
    g = lax.axis_index("leaf")
    up, down = lax.rem(s + sections - 1, sections), lax.rem(s + 1, sections)
    after, before = lax.rem(g + 1, groups), lax.rem(g + groups - 1, groups)
    parents = ({"section": up, "leaf": g}, {"section": up, "leaf": after})
    children = ({"section": down, "leaf": g}, {"section": down, "leaf": before})
    siblings = ({"leaf": after}, {"leaf": before})
    far_side = lax.rem(s, 2) == 1

    barrier = pltpu.get_barrier_semaphore()
    for other in children + siblings[1:]:
        pl.semaphore_signal(barrier, inc=1, device_id=other, device_id_type=MESH)

    @pl.when(s > 0)
    def _():
        pl.semaphore_signal(barrier, inc=1, device_id={"section": 0}, device_id_type=MESH)
        pl.semaphore_wait(barrier, 3)

    @pl.when(s == 0)
    def _():
        @pl.loop(1, groups)
        def _(d):
            pl.semaphore_signal(
                barrier, inc=1, device_id={"leaf": lax.rem(g + d, groups)}, device_id_type=MESH
            )

        pl.semaphore_wait(barrier, 3 + (groups - 1) + (sections - 1))

    def pieces(src, dst, send, recv, device):
        return [
            pltpu.make_async_remote_copy(
                src_ref=src.at[pl.ds(start, size)], dst_ref=dst.at[pl.ds(start, size)],
                send_sem=send.at[0], recv_sem=recv.at[i], device_id=device, device_id_type=MESH,
            )
            for i, (start, size) in enumerate(PIECES)
        ]

    def whole(src, dst, send, recv, device):
        return pltpu.make_async_remote_copy(
            src_ref=src, dst_ref=dst, send_sem=send.at[0], recv_sem=recv.at[0],
            device_id=device, device_id_type=MESH,
        )

    own_copies = pieces(own_out, own_in, own_send, own_recv, parents[0])
    far_copies = pieces(far_out, far_in, far_send, far_recv, parents[1])
    peer_copies = pieces(far_out, peer_in, peer_send, peer_recv, siblings[0])

    for i in range(4):
        block = slice(128 * i, 128 * (i + 1))
        value = state_map[block, :]
        m_s[0, block, :], m_s[1, block, :] = split(value)
        mt_s[0, :, block], mt_s[1, :, block] = split(value.T)
        value = input_map[block, :]
        n_s[0, block, :], n_s[1, block, :] = split(value)
        nt_s[0, :, block], nt_s[1, :, block] = split(value.T)

    @pl.when(s == 0)
    def _():
        fetch_m = pltpu.make_async_copy(root_state_map, mr_ref, local.at[0])
        fetch_n = pltpu.make_async_copy(root_input_map, nr_ref, local.at[1])
        fetch_m.start()
        fetch_n.start()
        fetch_m.wait()
        fetch_n.wait()
        for i in range(4):
            block = slice(128 * i, 128 * (i + 1))
            mr_s[0, block, :], mr_s[1, block, :] = split(mr_ref[block, :])
            value = nr_ref[block, :]
            nr_s[0, block, :], nr_s[1, block, :] = split(value)
            nrt_s[0, :, block], nrt_s[1, :, block] = split(value.T)
            column = jnp.sum(eye_times(root_terminal[0:1, block], 128), axis=1, keepdims=True)
            tail_ref[block, :] = column * value

    @pl.when(s == sections - 1)
    def _():
        own_in[...] = jnp.zeros_like(own_in)

    @pl.when(far_side)
    def _():
        far_in[...] = jnp.zeros_like(far_in)

    r = lax.broadcasted_iota(jnp.int32, (128, 128), 0)
    c = lax.broadcasted_iota(jnp.int32, (128, 128), 1)

    top, bottom = slice(0, 256), slice(256, 512)

    def both(ref, rowb, colb):
        return ref[0, rowb, colb], ref[1, rowb, colb]

    def put(i, j, block):
        rowb, colb = slice(128 * i, 128 * (i + 1)), slice(128 * j, 128 * (j + 1))
        if i == j:
            block = block + eye_times(terminal[0:1, rowb], 128)
        e_s[0, rowb, colb], e_s[1, rowb, colb] = split(block)
        if i != j:
            e_s[0, colb, rowb], e_s[1, colb, rowb] = split(block.T)

    for p, (start, size) in enumerate(PIECES):
        @pl.when(s < sections - 1)
        def _():
            own_copies[p].wait_recv()

            @pl.when(jnp.logical_not(far_side))
            def _():
                far_copies[p].wait_recv()

        for h, (kind, i, j) in enumerate(CONTENT[p]):
            here = slice(start + 128 * h, start + 128 * (h + 1))
            block = own_in[here, :] + far_in[here, :]
            if kind == "pair":
                spare = slice(start + 256, start + 257)
                line = own_in[spare, :] + far_in[spare, :]
                turned = block.T
                put(i, i, jnp.where(r >= c, block, turned))
                put(j, j, jnp.where(r < c, block, jnp.where(r > c, turned, line)))
            else:
                put(i, j, block)

        if p == 2:
            upper = dot_split(both(e_s, top, slice(None)), both(n_s, slice(None), slice(None)))
            yn_s[0, top, :], yn_s[1, top, :] = split(upper)
            yb_ref[:, 512:768] = dot_split(both(e_s, bottom, top), both(n_s, top, slice(None)))
            for colb in (slice(0, 256), slice(256, 512)):
                upper = dot_split(both(e_s, top, slice(None)), both(m_s, slice(None), colb))
                ym_s[0, top, colb], ym_s[1, top, colb] = split(upper)
                yb_ref[:, colb] = dot_split(both(e_s, bottom, top), both(m_s, top, colb))

    lower = yb_ref[:, 512:768] + dot_split(both(e_s, bottom, bottom), both(n_s, bottom, slice(None)))
    yn_s[0, bottom, :], yn_s[1, bottom, :] = split(lower)
    for colb in (slice(0, 256), slice(256, 512)):
        lower = yb_ref[:, colb] + dot_split(both(e_s, bottom, bottom), both(m_s, bottom, colb))
        ym_s[0, bottom, colb], ym_s[1, bottom, colb] = split(lower)
    nt, mt = (nt_s[0], nt_s[1]), (mt_s[0], mt_s[1])
    huu = dot_split(nt, (yn_s[0], yn_s[1])) + eye_times(cost_input[0:1, :], 256)
    for j in range(2):
        colb = slice(256 * j, 256 * (j + 1))
        hux_ref[:, colb] = dot_split(nt, (ym_s[0, :, colb], ym_s[1, :, colb]))
    for i in range(2):
        rowb = slice(256 * i, 256 * (i + 1))
        colb = slice(0, 256 * (i + 1))
        hess_ref[rowb, colb] = dot_split(
            (mt_s[0, rowb, :], mt_s[1, rowb, :]), (ym_s[0, :, colb], ym_s[1, :, colb])
        )

    hux1, th, rest, g2, g1 = solve(huu, hux_ref[...], inverse128)
    x_ref[0, 0:128, :], x_ref[1, 0:128, :] = split(hux1)
    x_ref[0, 128:256, :], x_ref[1, 128:256, :] = split(rest)
    z_ref[0, 0:128, :], z_ref[1, 0:128, :] = split(th)
    z_ref[0, 128:256, :], z_ref[1, 128:256, :] = split(g2)
    weight = prob[0].astype(F32) / 64.0
    crossing = crosses[0].astype(F32)
    far_weight = weight * crossing
    own_weight = weight - far_weight

    def load(start, value):
        far_out[start : start + value.shape[0], :] = value * far_weight
        own_out[start : start + value.shape[0], :] = value * own_weight

    for i in range(2):
        rowc = slice(256 * i, 256 * (i + 1))
        colc = slice(0, 256 * (i + 1))
        update = dot_split(
            (x_ref[0, :, rowc], x_ref[1, :, rowc]), (z_ref[0, :, colc], z_ref[1, :, colc]), CONTRACT_ROWS
        )
        for h in range(2):
            k = 2 * i + h
            rowb, colb = slice(128 * k, 128 * (k + 1)), slice(0, 128 * (k + 1))
            hess_ref[rowb, colb] = hess_ref[rowb, colb] - update[128 * h : 128 * (h + 1), 0 : 128 * (k + 1)]
            hess_ref[rowb, rowb] = hess_ref[rowb, rowb] + eye_times(cost_state[0:1, rowb], 128)
        for p in ((0,), (1, 2, 3))[i]:
            start = PIECES[p][0]
            for h, (kind, a, b) in enumerate(CONTENT[p]):
                block = hess_ref[128 * a : 128 * (a + 1), 128 * b : 128 * (b + 1)]
                if kind == "pair":
                    first = hess_ref[128 * a : 128 * (a + 1), 128 * a : 128 * (a + 1)]
                    second = hess_ref[128 * b : 128 * (b + 1), 128 * b : 128 * (b + 1)]
                    block = jnp.where(r >= c, first, second)
                    line = jnp.sum(jnp.where(r == c, second, 0.0), axis=0, keepdims=True)
                    load(start + 256, jnp.broadcast_to(line, (8, 128)))
                load(start + 128 * h, block)

            @pl.when(far_side)
            def _():
                far_copies[p].start()
                own_copies[p].start()

            @pl.when(jnp.logical_not(far_side) & (s > 0))
            def _():
                peer_copies[p].start()

    @pl.when(jnp.logical_not(far_side) & (s > 0))
    def _():
        for p, (start, size) in enumerate(PIECES):
            peer_copies[p].wait_recv()
            here = slice(start, start + size)
            own_out[here, :] = own_out[here, :] + peer_in[here, :]
            own_copies[p].start()

    for i in range(4):
        rowb = slice(128 * i, 128 * (i + 1))
        for j in range(i):
            colb = slice(128 * j, 128 * (j + 1))
            hess_ref[colb, rowb] = hess_ref[rowb, colb].T
    gain_ref[0:128, :] = -g1
    gain_ref[128:256, :] = -g2

    hess_write = pltpu.make_async_copy(hess_ref, hess_hbm, local.at[2])
    gain_write = pltpu.make_async_copy(gain_ref, gain_hbm, local.at[3])
    hess_write.start()
    gain_write.start()

    @pl.when(s > 0)
    def _():
        whole(own_out, own_in, own_send, own_recv, parents[0]).wait_send()

        @pl.when(far_side)
        def _():
            whole(far_out, far_in, far_send, far_recv, parents[1]).wait_send()

        @pl.when(jnp.logical_not(far_side))
        def _():
            whole(far_out, peer_in, peer_send, peer_recv, siblings[0]).wait_send()

    def part_copy(src, dst, peer):
        return pltpu.make_async_remote_copy(
            src_ref=part_ref.at[src], dst_ref=parts_in.at[dst], send_sem=part_send.at[0], recv_sem=part_recv.at[0],
            device_id={"leaf": peer}, device_id_type=MESH,
        )

    def full_copy(here, peer):
        return pltpu.make_async_remote_copy(
            src_ref=full_ref.at[here], dst_ref=full_ref.at[here], send_sem=full_send.at[0], recv_sem=full_recv.at[0],
            device_id={"leaf": peer}, device_id_type=MESH,
        )

    others = pl.ds(0, groups - 1)
    depth = part_ref.shape[1]

    def slice_copy(other):
        return pltpu.make_async_remote_copy(
            src_ref=slices_ref.at[other], dst_ref=slice_ref, send_sem=slice_send.at[0], recv_sem=slice_recv.at[0],
            device_id={"section": other}, device_id_type=MESH,
        )

    @pl.when(s == 0)
    def _():
        nr = (nr_s[0], nr_s[1])
        for i in range(2):
            rowb = slice(256 * i, 256 * (i + 1))
            product = dot_split(split(hess_ref[rowb, :]), nr) * weight
            for j in range(256 // depth):
                part_ref[i * (256 // depth) + j] = product[depth * j : depth * (j + 1)]

        @pl.loop(1, groups)
        def _(d):
            peer = lax.rem(g + d, groups)
            part_copy(peer, g, peer).start()

        parts_in[g] = part_ref[g]
        part_copy(others, others, siblings[0]["leaf"]).wait_recv()
        total = tail_ref[pl.ds(pl.multiple_of(depth * g, depth), depth), :]
        for i in range(groups):
            total = total + parts_in[i]
        full_ref[g] = total

        @pl.loop(1, groups)
        def _(d):
            full_copy(g, lax.rem(g + d, groups)).start()

        full_copy(others, siblings[0]["leaf"]).wait_recv()
        y = split(full_ref[...].reshape(groups * depth, full_ref.shape[2]))
        root_huu = dot_split((nrt_s[0], nrt_s[1]), y) + eye_times(root_cost_input[0:1, :], 256)
        root_hux = dot_split(y, (mr_s[0], mr_s[1]), CONTRACT_ROWS)
        _, _, _, low, high = solve(root_huu, root_hux, inverse128)
        for i in range(sections):
            half, start = (-high, -low)[i // (sections // 2)], 32 * (i % (sections // 2))
            slices_ref[i] = half[start : start + 32]

        @pl.loop(1, sections)
        def _(d):
            slice_copy(d).start()

        root_ref[...] = slices_ref[0]
        part_copy(others, others, siblings[0]["leaf"]).wait_send()
        full_copy(others, siblings[0]["leaf"]).wait_send()
        pltpu.make_async_remote_copy(
            src_ref=slices_ref.at[pl.ds(1, sections - 1)], dst_ref=slices_ref.at[pl.ds(1, sections - 1)],
            send_sem=slice_send.at[0], recv_sem=slice_recv.at[0],
            device_id={"section": 1}, device_id_type=MESH,
        ).wait_send()

    @pl.when(s > 0)
    def _():
        slice_copy(s).wait_recv()
        root_ref[...] = slice_ref[...]

    hess_write.wait()
    gain_write.wait()


def on_device(
    state_map, input_map, cost_state, cost_input, terminal, prob_num, crosses,
    root_state_map, root_input_map, root_cost_input, root_terminal,
):
    sections, groups = lax.axis_size("section"), lax.axis_size("leaf")
    nx, nu = input_map.shape[1], input_map.shape[2]
    vmem, smem = pl.BlockSpec(memory_space=pltpu.VMEM), pl.BlockSpec(memory_space=pltpu.SMEM)
    hbm = pl.BlockSpec(memory_space=pl.ANY)
    dma = pltpu.SemaphoreType.DMA
    hess, gain, mine = pl.pallas_call(
        functools.partial(chain_kernel, sections, groups),
        out_shape=(
            jax.ShapeDtypeStruct((nx, nx), F32),
            jax.ShapeDtypeStruct((nu, nx), F32),
            jax.ShapeDtypeStruct((nu // sections, nx), F32),
        ),
        in_specs=[smem, smem] + [vmem] * 5 + [hbm, hbm, vmem, vmem],
        out_specs=(hbm, hbm, vmem),
        scratch_shapes=[VMEM((nx, nx), F32), VMEM((nu, nx), F32)]
        + [VMEM((1040, 128), F32)] * 5
        + [
            VMEM((2, nx, nx), BF16), VMEM((2, nx, nu), BF16), VMEM((2, nx, nx), BF16), VMEM((2, nu, nx), BF16),
            VMEM((2, nx, nx), BF16), VMEM((2, nx, nx), BF16), VMEM((2, nx, nu), BF16),
            VMEM((nu, nx), F32), VMEM((2, nu, nx), BF16), VMEM((2, nu, nx), BF16), VMEM((nx // 2, nx + nu), F32),
            VMEM((nx, nx), F32), VMEM((nx, nu), F32), VMEM((2, nx, nx), BF16), VMEM((2, nx, nu), BF16),
            VMEM((2, nu, nx), BF16), VMEM((nx, nu), F32)]
        + [VMEM((groups, nx // groups, nu), F32)] * 3
        + [
            VMEM((sections, nu // sections, nx), F32), VMEM((nu // sections, nx), F32),
        ]
        + [dma((1,)), dma((4,))] * 3
        + [dma((1,))] * 6
        + [dma((4,))],
        compiler_params=pltpu.CompilerParams(collective_id=0, has_side_effects=True, vmem_limit_bytes=60 << 20),
    )(
        prob_num.reshape(1), crosses.reshape(1), state_map[0], input_map[0],
        cost_state.reshape(1, nx), cost_input.reshape(1, nu), terminal.reshape(1, nx),
        root_state_map, root_input_map, root_cost_input, root_terminal,
    )
    return hess[None, None, None], gain[None, None, None], mine[None]


def solution(mesh):
    in_specs = (
        P("section", None, None), P("section", None, None), P("section", None, "leaf", None),
        P("section", None, "leaf", None), P("section", None, "leaf", None), P("section", None, "leaf"),
        P("section", None, "leaf"), P(), P(), P(), P(),
    )
    out_specs = (
        P("section", None, "leaf", None, None), P("section", None, "leaf", None, None), P(None, "section", None),
    )
    return jax.shard_map(on_device, mesh=mesh, in_specs=in_specs, out_specs=out_specs, check_vma=False)
```

```python
import functools

import jax
import jax.numpy as jnp
from jax import lax
from jax.experimental import pallas as pl
from jax.experimental.pallas import tpu as pltpu
from jax.sharding import PartitionSpec as P

F32, BF16 = jnp.float32, jnp.bfloat16
PIECES = ((0, 264), (264, 256), (520, 256), (776, 136), (912, 128))
CONTENT = (
    (("pair", 0, 1), ("one", 1, 0)), (("one", 2, 0), ("one", 2, 1)), (("one", 3, 0), ("one", 3, 1)),
    (("pair", 2, 3),), (("one", 3, 2),),
)
MESH = pl.DeviceIdType.MESH
VMEM = pltpu.VMEM
CONTRACT = (((1,), (0,)), ((), ()))
CONTRACT_ROWS = (((0,), (0,)), ((), ()))


def split(x):
    high = x.astype(BF16)
    return high, (x - high.astype(F32)).astype(BF16)


def dot_one(a, b, dims=CONTRACT):
    return lax.dot_general(a, b, dims, preferred_element_type=F32)


def dot_split(a, b, dims=CONTRACT):
    return dot_one(a[0], b[0], dims) + (dot_one(a[0], b[1], dims) + dot_one(a[1], b[0], dims))


def dot3(a, b, dims=CONTRACT):
    return dot_split(split(a), split(b), dims)


def lanes(x, j):
    return jnp.broadcast_to(x[:, j : j + 1], (8, 128))


def rows(x, k):
    return jnp.broadcast_to(x[k : k + 1, :], (8, 128))


def inverse128(a):
    groups = 16
    lane = lax.broadcasted_iota(jnp.int32, (8, 128), 1)
    row = lax.broadcasted_iota(jnp.int32, (8, 128), 0)
    masks = [row == k for k in range(8)]
    held = [a[8 * g : 8 * g + 8, :] for g in range(groups)]
    for t in range(groups):
        off = 8 * t
        inside = (lane >= off) & (lane < off + 8)
        top = held[t]
        cols = [lanes(top, off + j) for j in range(8)]
        top = jnp.where(inside, jnp.where(lane - off == row, 1.0, 0.0), top)
        for k in range(8):
            pivot = 1.0 / rows(cols[k], k)
            lead = rows(top, k) * pivot
            factor = jnp.where(masks[k], 0.0, cols[k])
            top = jnp.where(masks[k], lead, top - factor * lead)
            for j in range(k + 1, 8):
                lead_j = rows(cols[j], k) * pivot
                cols[j] = jnp.where(masks[k], lead_j, cols[j] - factor * lead_j)
        out = [jnp.where(inside, 0.0, held[g]) for g in range(groups)]
        for k in range(8):
            lead = rows(top, k)
            for g in range(groups):
                if g != t:
                    out[g] = out[g] - lanes(held[g], off + k) * lead
        out[t] = top
        held = out
    return jnp.concatenate(held, axis=0)


def solve(huu, hux, inv):
    a12, a21 = huu[0:128, 128:256], huu[128:256, 0:128]
    hux1 = hux[0:128]
    first = split(inv(huu[0:128, 0:128]))
    t12 = dot_split(first, split(a12))
    th = dot_split(first, split(hux1))
    a21s = split(a21)
    second = split(inv(huu[128:256, 128:256] - dot_split(a21s, split(t12))))
    rest = hux[128:256] - dot_split(a21s, split(th))
    g2 = dot_split(second, split(rest))
    g1 = th - dot3(t12, g2)
    return hux1, th, rest, g2, g1


def eye_times(vector, size):
    r = lax.broadcasted_iota(jnp.int32, (size, size), 0)
    c = lax.broadcasted_iota(jnp.int32, (size, size), 1)
    return jnp.where(r == c, jnp.broadcast_to(vector, (size, size)), 0.0)


def chain_kernel(
    sections, groups, prob, crosses, state_map, input_map, cost_state, cost_input, terminal,
    root_state_map, root_input_map, root_cost_input, root_terminal,
    hess_hbm, gain_hbm, root_ref,
    hess_ref, gain_ref, own_in, far_in, peer_in, own_out, far_out,
    m_s, n_s, mt_s, nt_s, e_s, ym_s, yn_s, hux_ref, z_ref, x_ref, yb_ref,
    mr_ref, nr_ref, mr_s, nr_s, nrt_s, tail_ref, part_ref, parts_in, full_ref, slices_ref, slice_ref,
    own_send, own_recv, far_send, far_recv, peer_send, peer_recv,
    part_send, part_recv, full_send, full_recv, slice_send, slice_recv, local,
):
    s = lax.axis_index("section")
    g = lax.axis_index("leaf")
    up, down = lax.rem(s + sections - 1, sections), lax.rem(s + 1, sections)
    after, before = lax.rem(g + 1, groups), lax.rem(g + groups - 1, groups)
    parents = ({"section": up, "leaf": g}, {"section": up, "leaf": after})
    children = ({"section": down, "leaf": g}, {"section": down, "leaf": before})
    siblings = ({"leaf": after}, {"leaf": before})
    far_side = lax.rem(s, 2) == 1

    barrier = pltpu.get_barrier_semaphore()
    for other in children + siblings[1:]:
        pl.semaphore_signal(barrier, inc=1, device_id=other, device_id_type=MESH)

    @pl.when(s > 0)
    def _():
        pl.semaphore_signal(barrier, inc=1, device_id={"section": 0}, device_id_type=MESH)
        pl.semaphore_wait(barrier, 3)

    @pl.when(s == 0)
    def _():
        @pl.loop(1, groups)
        def _(d):
            pl.semaphore_signal(
                barrier, inc=1, device_id={"leaf": lax.rem(g + d, groups)}, device_id_type=MESH
            )

        pl.semaphore_wait(barrier, 3 + (groups - 1) + (sections - 1))

    def pieces(src, dst, send, recv, device):
        return [
            pltpu.make_async_remote_copy(
                src_ref=src.at[pl.ds(start, size)], dst_ref=dst.at[pl.ds(start, size)],
                send_sem=send.at[0], recv_sem=recv.at[i], device_id=device, device_id_type=MESH,
            )
            for i, (start, size) in enumerate(PIECES)
        ]

    def whole(src, dst, send, recv, device):
        return pltpu.make_async_remote_copy(
            src_ref=src, dst_ref=dst, send_sem=send.at[0], recv_sem=recv.at[0],
            device_id=device, device_id_type=MESH,
        )

    own_copies = pieces(own_out, own_in, own_send, own_recv, parents[0])
    far_copies = pieces(far_out, far_in, far_send, far_recv, parents[1])
    peer_copies = pieces(far_out, peer_in, peer_send, peer_recv, siblings[0])

    for i in range(4):
        block = slice(128 * i, 128 * (i + 1))
        value = state_map[block, :]
        m_s[0, block, :], m_s[1, block, :] = split(value)
        mt_s[0, :, block], mt_s[1, :, block] = split(value.T)
        value = input_map[block, :]
        n_s[0, block, :], n_s[1, block, :] = split(value)
        nt_s[0, :, block], nt_s[1, :, block] = split(value.T)

    @pl.when(s == 0)
    def _():
        fetch_m = pltpu.make_async_copy(root_state_map, mr_ref, local.at[0])
        fetch_n = pltpu.make_async_copy(root_input_map, nr_ref, local.at[1])
        fetch_m.start()
        fetch_n.start()
        fetch_m.wait()
        fetch_n.wait()
        for i in range(4):
            block = slice(128 * i, 128 * (i + 1))
            mr_s[0, block, :], mr_s[1, block, :] = split(mr_ref[block, :])
            value = nr_ref[block, :]
            nr_s[0, block, :], nr_s[1, block, :] = split(value)
            nrt_s[0, :, block], nrt_s[1, :, block] = split(value.T)
            column = jnp.sum(eye_times(root_terminal[0:1, block], 128), axis=1, keepdims=True)
            tail_ref[block, :] = column * value

    @pl.when(s == sections - 1)
    def _():
        own_in[...] = jnp.zeros_like(own_in)

    @pl.when(far_side)
    def _():
        far_in[...] = jnp.zeros_like(far_in)

    r = lax.broadcasted_iota(jnp.int32, (128, 128), 0)
    c = lax.broadcasted_iota(jnp.int32, (128, 128), 1)

    top, bottom = slice(0, 256), slice(256, 512)

    def both(ref, rowb, colb):
        return ref[0, rowb, colb], ref[1, rowb, colb]

    def put(i, j, block):
        rowb, colb = slice(128 * i, 128 * (i + 1)), slice(128 * j, 128 * (j + 1))
        if i == j:
            block = block + eye_times(terminal[0:1, rowb], 128)
        e_s[0, rowb, colb], e_s[1, rowb, colb] = split(block)
        if i != j:
            e_s[0, colb, rowb], e_s[1, colb, rowb] = split(block.T)

    for p, (start, size) in enumerate(PIECES):
        @pl.when(s < sections - 1)
        def _():
            own_copies[p].wait_recv()

            @pl.when(jnp.logical_not(far_side))
            def _():
                far_copies[p].wait_recv()

        for h, (kind, i, j) in enumerate(CONTENT[p]):
            here = slice(start + 128 * h, start + 128 * (h + 1))
            block = own_in[here, :] + far_in[here, :]
            if kind == "pair":
                spare = slice(start + size - 8, start + size - 7)
                line = own_in[spare, :] + far_in[spare, :]
                turned = block.T
                put(i, i, jnp.where(r >= c, block, turned))
                put(j, j, jnp.where(r < c, block, jnp.where(r > c, turned, line)))
            else:
                put(i, j, block)

        if p == 2:
            upper = dot_split(both(e_s, top, slice(None)), both(n_s, slice(None), slice(None)))
            yn_s[0, top, :], yn_s[1, top, :] = split(upper)
            yb_ref[:, 512:768] = dot_split(both(e_s, bottom, top), both(n_s, top, slice(None)))
            for colb in (slice(0, 256), slice(256, 512)):
                upper = dot_split(both(e_s, top, slice(None)), both(m_s, slice(None), colb))
                ym_s[0, top, colb], ym_s[1, top, colb] = split(upper)
                yb_ref[:, colb] = dot_split(both(e_s, bottom, top), both(m_s, top, colb))

    lower = yb_ref[:, 512:768] + dot_split(both(e_s, bottom, bottom), both(n_s, bottom, slice(None)))
    yn_s[0, bottom, :], yn_s[1, bottom, :] = split(lower)
    for colb in (slice(0, 256), slice(256, 512)):
        lower = yb_ref[:, colb] + dot_split(both(e_s, bottom, bottom), both(m_s, bottom, colb))
        ym_s[0, bottom, colb], ym_s[1, bottom, colb] = split(lower)
    nt, mt = (nt_s[0], nt_s[1]), (mt_s[0], mt_s[1])
    huu = dot_split(nt, (yn_s[0], yn_s[1])) + eye_times(cost_input[0:1, :], 256)
    for j in range(2):
        colb = slice(256 * j, 256 * (j + 1))
        hux_ref[:, colb] = dot_split(nt, (ym_s[0, :, colb], ym_s[1, :, colb]))
    for i in range(2):
        rowb = slice(256 * i, 256 * (i + 1))
        colb = slice(0, 256 * (i + 1))
        hess_ref[rowb, colb] = dot_split(
            (mt_s[0, rowb, :], mt_s[1, rowb, :]), (ym_s[0, :, colb], ym_s[1, :, colb])
        )

    hux1, th, rest, g2, g1 = solve(huu, hux_ref[...], inverse128)
    x_ref[0, 0:128, :], x_ref[1, 0:128, :] = split(hux1)
    x_ref[0, 128:256, :], x_ref[1, 128:256, :] = split(rest)
    z_ref[0, 0:128, :], z_ref[1, 0:128, :] = split(th)
    z_ref[0, 128:256, :], z_ref[1, 128:256, :] = split(g2)
    weight = prob[0].astype(F32) / 64.0
    crossing = crosses[0].astype(F32)
    far_weight = weight * crossing
    own_weight = weight - far_weight

    def load(start, value):
        far_out[start : start + value.shape[0], :] = value * far_weight
        own_out[start : start + value.shape[0], :] = value * own_weight

    for i in range(2):
        rowc = slice(256 * i, 256 * (i + 1))
        colc = slice(0, 256 * (i + 1))
        update = dot_split(
            (x_ref[0, :, rowc], x_ref[1, :, rowc]), (z_ref[0, :, colc], z_ref[1, :, colc]), CONTRACT_ROWS
        )
        for h in range(2):
            k = 2 * i + h
            rowb, colb = slice(128 * k, 128 * (k + 1)), slice(0, 128 * (k + 1))
            hess_ref[rowb, colb] = hess_ref[rowb, colb] - update[128 * h : 128 * (h + 1), 0 : 128 * (k + 1)]
            hess_ref[rowb, rowb] = hess_ref[rowb, rowb] + eye_times(cost_state[0:1, rowb], 128)
        for p in ((0,), (1, 2, 3, 4))[i]:
            start, size = PIECES[p]
            for h, (kind, a, b) in enumerate(CONTENT[p]):
                block = hess_ref[128 * a : 128 * (a + 1), 128 * b : 128 * (b + 1)]
                if kind == "pair":
                    first = hess_ref[128 * a : 128 * (a + 1), 128 * a : 128 * (a + 1)]
                    second = hess_ref[128 * b : 128 * (b + 1), 128 * b : 128 * (b + 1)]
                    block = jnp.where(r >= c, first, second)
                    line = jnp.sum(jnp.where(r == c, second, 0.0), axis=0, keepdims=True)
                    load(start + size - 8, jnp.broadcast_to(line, (8, 128)))
                load(start + 128 * h, block)

            @pl.when(far_side)
            def _():
                far_copies[p].start()
                own_copies[p].start()

            @pl.when(jnp.logical_not(far_side) & (s > 0))
            def _():
                peer_copies[p].start()

    @pl.when(jnp.logical_not(far_side) & (s > 0))
    def _():
        for p, (start, size) in enumerate(PIECES):
            peer_copies[p].wait_recv()
            here = slice(start, start + size)
            own_out[here, :] = own_out[here, :] + peer_in[here, :]
            own_copies[p].start()

    for i in range(4):
        rowb = slice(128 * i, 128 * (i + 1))
        for j in range(i):
            colb = slice(128 * j, 128 * (j + 1))
            hess_ref[colb, rowb] = hess_ref[rowb, colb].T
    gain_ref[0:128, :] = -g1
    gain_ref[128:256, :] = -g2

    hess_write = pltpu.make_async_copy(hess_ref, hess_hbm, local.at[2])
    gain_write = pltpu.make_async_copy(gain_ref, gain_hbm, local.at[3])
    hess_write.start()
    gain_write.start()

    @pl.when(s > 0)
    def _():
        whole(own_out, own_in, own_send, own_recv, parents[0]).wait_send()

        @pl.when(far_side)
        def _():
            whole(far_out, far_in, far_send, far_recv, parents[1]).wait_send()

        @pl.when(jnp.logical_not(far_side))
        def _():
            whole(far_out, peer_in, peer_send, peer_recv, siblings[0]).wait_send()

    def part_copy(src, dst, peer):
        return pltpu.make_async_remote_copy(
            src_ref=part_ref.at[src], dst_ref=parts_in.at[dst], send_sem=part_send.at[0], recv_sem=part_recv.at[0],
            device_id={"leaf": peer}, device_id_type=MESH,
        )

    def full_copy(here, peer):
        return pltpu.make_async_remote_copy(
            src_ref=full_ref.at[here], dst_ref=full_ref.at[here], send_sem=full_send.at[0], recv_sem=full_recv.at[0],
            device_id={"leaf": peer}, device_id_type=MESH,
        )

    others = pl.ds(0, groups - 1)
    depth = part_ref.shape[1]

    def slice_copy(other):
        return pltpu.make_async_remote_copy(
            src_ref=slices_ref.at[other], dst_ref=slice_ref, send_sem=slice_send.at[0], recv_sem=slice_recv.at[0],
            device_id={"section": other}, device_id_type=MESH,
        )

    @pl.when(s == 0)
    def _():
        nr = (nr_s[0], nr_s[1])
        for i in range(2):
            rowb = slice(256 * i, 256 * (i + 1))
            product = dot_split(split(hess_ref[rowb, :]), nr) * weight
            for j in range(256 // depth):
                part_ref[i * (256 // depth) + j] = product[depth * j : depth * (j + 1)]

        @pl.loop(1, groups)
        def _(d):
            peer = lax.rem(g + d, groups)
            part_copy(peer, g, peer).start()

        parts_in[g] = part_ref[g]
        part_copy(others, others, siblings[0]["leaf"]).wait_recv()
        total = tail_ref[pl.ds(pl.multiple_of(depth * g, depth), depth), :]
        for i in range(groups):
            total = total + parts_in[i]
        full_ref[g] = total

        @pl.loop(1, groups)
        def _(d):
            full_copy(g, lax.rem(g + d, groups)).start()

        full_copy(others, siblings[0]["leaf"]).wait_recv()
        y = split(full_ref[...].reshape(groups * depth, full_ref.shape[2]))
        root_huu = dot_split((nrt_s[0], nrt_s[1]), y) + eye_times(root_cost_input[0:1, :], 256)
        root_hux = dot_split(y, (mr_s[0], mr_s[1]), CONTRACT_ROWS)
        _, _, _, low, high = solve(root_huu, root_hux, inverse128)
        for i in range(sections):
            half, start = (-high, -low)[i // (sections // 2)], 32 * (i % (sections // 2))
            slices_ref[i] = half[start : start + 32]

        @pl.loop(1, sections)
        def _(d):
            slice_copy(d).start()

        root_ref[...] = slices_ref[0]
        part_copy(others, others, siblings[0]["leaf"]).wait_send()
        full_copy(others, siblings[0]["leaf"]).wait_send()
        pltpu.make_async_remote_copy(
            src_ref=slices_ref.at[pl.ds(1, sections - 1)], dst_ref=slices_ref.at[pl.ds(1, sections - 1)],
            send_sem=slice_send.at[0], recv_sem=slice_recv.at[0],
            device_id={"section": 1}, device_id_type=MESH,
        ).wait_send()

    @pl.when(s > 0)
    def _():
        slice_copy(s).wait_recv()
        root_ref[...] = slice_ref[...]

    hess_write.wait()
    gain_write.wait()


def on_device(
    state_map, input_map, cost_state, cost_input, terminal, prob_num, crosses,
    root_state_map, root_input_map, root_cost_input, root_terminal,
):
    sections, groups = lax.axis_size("section"), lax.axis_size("leaf")
    nx, nu = input_map.shape[1], input_map.shape[2]
    vmem, smem = pl.BlockSpec(memory_space=pltpu.VMEM), pl.BlockSpec(memory_space=pltpu.SMEM)
    hbm = pl.BlockSpec(memory_space=pl.ANY)
    dma = pltpu.SemaphoreType.DMA
    hess, gain, mine = pl.pallas_call(
        functools.partial(chain_kernel, sections, groups),
        out_shape=(
            jax.ShapeDtypeStruct((nx, nx), F32),
            jax.ShapeDtypeStruct((nu, nx), F32),
            jax.ShapeDtypeStruct((nu // sections, nx), F32),
        ),
        in_specs=[smem, smem] + [vmem] * 5 + [hbm, hbm, vmem, vmem],
        out_specs=(hbm, hbm, vmem),
        scratch_shapes=[VMEM((nx, nx), F32), VMEM((nu, nx), F32)]
        + [VMEM((1040, 128), F32)] * 5
        + [
            VMEM((2, nx, nx), BF16), VMEM((2, nx, nu), BF16), VMEM((2, nx, nx), BF16), VMEM((2, nu, nx), BF16),
            VMEM((2, nx, nx), BF16), VMEM((2, nx, nx), BF16), VMEM((2, nx, nu), BF16),
            VMEM((nu, nx), F32), VMEM((2, nu, nx), BF16), VMEM((2, nu, nx), BF16), VMEM((nx // 2, nx + nu), F32),
            VMEM((nx, nx), F32), VMEM((nx, nu), F32), VMEM((2, nx, nx), BF16), VMEM((2, nx, nu), BF16),
            VMEM((2, nu, nx), BF16), VMEM((nx, nu), F32)]
        + [VMEM((groups, nx // groups, nu), F32)] * 3
        + [
            VMEM((sections, nu // sections, nx), F32), VMEM((nu // sections, nx), F32),
        ]
        + [dma((1,)), dma((len(PIECES),))] * 3
        + [dma((1,))] * 6
        + [dma((4,))],
        compiler_params=pltpu.CompilerParams(collective_id=0, has_side_effects=True, vmem_limit_bytes=60 << 20),
    )(
        prob_num.reshape(1), crosses.reshape(1), state_map[0], input_map[0],
        cost_state.reshape(1, nx), cost_input.reshape(1, nu), terminal.reshape(1, nx),
        root_state_map, root_input_map, root_cost_input, root_terminal,
    )
    return hess[None, None, None], gain[None, None, None], mine[None]


def solution(mesh):
    in_specs = (
        P("section", None, None), P("section", None, None), P("section", None, "leaf", None),
        P("section", None, "leaf", None), P("section", None, "leaf", None), P("section", None, "leaf"),
        P("section", None, "leaf"), P(), P(), P(), P(),
    )
    out_specs = (
        P("section", None, "leaf", None, None), P("section", None, "leaf", None, None), P(None, "section", None),
    )
    return jax.shard_map(on_device, mesh=mesh, in_specs=in_specs, out_specs=out_specs, check_vma=False)
```
